256 devices in a mesh: gx: 4 (over x), gy: 8 (over z_lo, core), gz: 8 (over z_hi, y).
Axes of the slice: x: 4, y: 4, z: 8 (z_hi: 2, z_lo: 4; z = z_hi * 4 + z_lo), core: 2. Of those that a mesh axis runs over, the one named last changes fastest.
Arguments:
- features: bfloat16 [32, 32, 256, 1024], P(None, 'gx', 'gy', 'gz'), may hold values from -12 to 12
- posteriors: bfloat16 [16, 32, 256, 1024], P(None, 'gx', 'gy', 'gz'), may hold values from 0 to 1, as said below
Outputs:
- segmentation: bfloat16 [16, 32, 256, 1024], P(None, 'gx', 'gy', 'gz')
- class_means: float32 [16, 32], replicated
The draws below stay inside these ranges and needn't reach their ends.
Inputs may be any that keep to these rules, and one draw needn't show every extreme that they name: Each voxel's 16 initial posteriors are positive and sum to one up to rounding.
All inputs are finite; a program needn't handle non-finite values.
Results may differ from the reference program's by a relative error of at most 0.0075.
Values may be sent and summed in bfloat16 or wider, within the bound.
A program may use at most 128 MiB of HBM per device.

```python
import jax
import jax.numpy as jnp
from jax import lax

FEATS = 32
CLASSES = 16
SWEEPS = 2
VOXELS_ALONG_X = 32
VOXELS_ALONG_Y = 256
VOXELS_ALONG_Z = 1024


def class_labels(key):
    grid_shape = (VOXELS_ALONG_X, VOXELS_ALONG_Y, VOXELS_ALONG_Z)
    share = CLASSES // 4
    order = jax.random.permutation(jax.random.fold_in(key, 5), CLASSES).astype(jnp.int32)
    quarter = (jnp.arange(VOXELS_ALONG_X, dtype=jnp.int32) * 4 // VOXELS_ALONG_X)[:, None, None]
    eighth = (jnp.arange(VOXELS_ALONG_Z, dtype=jnp.int32) * 8 // VOXELS_ALONG_Z)[None, None, :]
    pick = jax.random.randint(jax.random.fold_in(key, 7), grid_shape, 0, share).astype(jnp.int32)
    coin = jax.random.randint(jax.random.fold_in(key, 8), grid_shape, 0, 2).astype(jnp.int32)
    pick = jnp.where(coin == 1, eighth % share + 0 * pick, pick)
    slot = quarter * share + pick
    return jnp.take(order, slot)


def draw_features(key, part):
    label = class_labels(key)
    centers = 1.2 * jax.random.normal(jax.random.fold_in(key, 11), (FEATS, CLASSES), jnp.float32)
    base = jnp.take(centers, label, axis=1)
    noise = jax.random.normal(jax.random.fold_in(key, 12), (FEATS, VOXELS_ALONG_X, VOXELS_ALONG_Y, VOXELS_ALONG_Z), jnp.float32)
    return jnp.clip(base + noise, -12.0, 12.0).astype(jnp.bfloat16)


def draw_posteriors(key, part):
    label = class_labels(key)
    onehot = (label[None] == jnp.arange(CLASSES, dtype=jnp.int32)[:, None, None, None]).astype(jnp.float32)
    noise = jax.random.normal(jax.random.fold_in(key, 14), (CLASSES, VOXELS_ALONG_X, VOXELS_ALONG_Y, VOXELS_ALONG_Z), jnp.float32)
    return jax.nn.softmax(1.5 * onehot + noise, axis=0).astype(jnp.bfloat16)


def setup_inputs(seed: int = 0) -> dict:
    streams_of = jax.random.split(jax.random.key(seed), 3)
    features = draw_features(jax.random.fold_in(streams_of[2], 71), 0)
    posteriors = draw_posteriors(jax.random.fold_in(streams_of[2], 71), 0)
    return {"features": features, "posteriors": posteriors}


beta_coupling = 1.0
ridge = 0.1

def finish(counts, total_weight, first_moment, scatter):
    identity = jnp.eye(first_moment.shape[1], dtype=jnp.float32)
    centers = first_moment / counts[:, None]
    spread = scatter / counts[:, None, None] - centers[:, :, None] * centers[:, None, :] + ridge * identity
    factor = jnp.linalg.cholesky(spread)
    whiten = jax.vmap(lambda lower_factor: jax.scipy.linalg.solve_triangular(lower_factor, identity, lower=True))(factor)
    offset = jnp.einsum('kgf,kf->kg', whiten, centers, precision=lax.Precision.HIGHEST)
    biases = jnp.log(counts / total_weight) - jnp.sum(jnp.log(jnp.diagonal(factor, axis1=1, axis2=2)), axis=1)
    return (centers, whiten, offset, biases)

def local_moments(posterior, voxels):
    flat_post = posterior.reshape(posterior.shape[0], -1)
    flat_vox = voxels.reshape(voxels.shape[0], -1)
    contract = (((1,), (1,)), ((), ()))
    counts = jnp.sum(flat_post.astype(jnp.float32), axis=1)
    first_moment = lax.dot_general(flat_post.astype(jnp.float32), flat_vox.astype(jnp.float32), contract, preferred_element_type=jnp.float32)

    def second(weights_row):
        weighted = weights_row[None, :] * flat_vox
        return lax.dot_general(weighted.astype(jnp.float32), flat_vox.astype(jnp.float32), contract, preferred_element_type=jnp.float32)
    scatter = lax.map(second, flat_post)
    return (counts, first_moment, scatter)

def loglik(voxels, whiten, offset, biases):
    flat_vox = voxels.reshape(voxels.shape[0], -1)
    rounded = whiten.astype(jnp.bfloat16)

    def per_class(class_record):
        matrix, shift, level = class_record
        whitened = jnp.dot(matrix.astype(jnp.float32), flat_vox.astype(jnp.float32), preferred_element_type=jnp.float32) - shift[:, None]
        return level - 0.5 * jnp.sum(whitened * whitened, axis=0)
    scores = lax.map(per_class, (rounded, offset, biases))
    return scores.reshape((whiten.shape[0],) + voxels.shape[1:])

def neighbours(padded):
    inner = padded[:, 2:, 1:-1, 1:-1] + padded[:, :-2, 1:-1, 1:-1]
    inner = inner + padded[:, 1:-1, 2:, 1:-1] + padded[:, 1:-1, :-2, 1:-1]
    return inner + padded[:, 1:-1, 1:-1, 2:] + padded[:, 1:-1, 1:-1, :-2]

def state_update(scores, near_sum):
    return jax.nn.softmax(scores + beta_coupling * near_sum, axis=0).astype(jnp.bfloat16)

def padded_of(posterior):
    return jnp.pad(posterior.astype(jnp.float32), ((0, 0), (1, 1), (1, 1), (1, 1)))

def reference(features, posteriors):
    counts, first_moment, scatter = local_moments(posteriors, features)
    centers, whiten, offset, biases = finish(counts, jnp.sum(counts), first_moment, scatter)
    scores = loglik(features, whiten, offset, biases)
    current = posteriors
    for pass_index in range(SWEEPS):
        current = state_update(scores, neighbours(padded_of(current)))
    counts, first_moment, scatter = local_moments(current, features)
    centers, whiten, offset, biases = finish(counts, jnp.sum(counts), first_moment, scatter)
    scores = loglik(features, whiten, offset, biases)
    segmentation = state_update(scores, neighbours(padded_of(current)))
    return (segmentation, centers)
```

```python
import functools

import jax
import jax.numpy as jnp
from jax import lax
from jax.experimental import pallas as pl
from jax.experimental.pallas import tpu as pltpu
from jax.sharding import PartitionSpec as P

SWEEPS = 2
FEATS = 32
CLASSES = 16
LANES = 128
GROUP = 8
PIECES = 8
PIECE_ROWS = 24
AUG = 48

beta_coupling = 1.0
ridge = 0.1

AXES = ("gx", "gy", "gz")
MESH = pl.DeviceIdType.MESH
VMEM = pl.BlockSpec(memory_space=pltpu.VMEM)
NT = (((1,), (1,)), ((), ()))


def augmented(rows):
    count = rows.shape[1]
    index = lax.broadcasted_iota(jnp.int32, (AUG - FEATS, count), 0)
    extra = jnp.where(index < 3, 1.0, 0.0).astype(jnp.bfloat16)
    return jnp.concatenate([rows, extra], axis=0)


def face_of(q_rows, low_ref, high_ref, step):
    side = lax.broadcasted_iota(jnp.int32, (16, LANES), 0)
    lane = lax.broadcasted_iota(jnp.int32, (16, LANES), 1)
    pick = ((side == 0) & (lane == 0)) | ((side == 1) & (lane == LANES - 1))
    pick = jnp.where(pick, 1.0, 0.0).astype(jnp.bfloat16)
    faces = lax.dot_general(pick, q_rows, NT, preferred_element_type=jnp.float32)
    width = GROUP * CLASSES
    where = pl.ds(pl.multiple_of(step * width, width), width)
    low_ref[:, where] = faces[0:1].astype(jnp.bfloat16)
    high_ref[:, where] = faces[1:2].astype(jnp.bfloat16)


def add_moments(rows, posts, total):
    weighted = []
    for row, post in zip(rows, posts):
        parts = [post[k : k + 1, :] * row for k in range(CLASSES)] + [post]
        weighted.append(jnp.concatenate(parts, axis=0))
    left = jnp.concatenate(weighted, axis=1)
    right = augmented(jnp.concatenate(rows, axis=1))
    total[:, :AUG] += lax.dot_general(left, right, NT, preferred_element_type=jnp.float32)


def pack_moments(total, out_ref):
    rows_per = FEATS // PIECES
    for piece in range(PIECES):
        blocks = []
        for r in range(rows_per):
            row = piece * rows_per + r
            blocks.append(total[pl.ds(row, CLASSES, stride=FEATS), :][:, :FEATS])
        out_ref[piece, :CLASSES, :] = jnp.concatenate(blocks, axis=1)
        if piece < 2:
            start = CLASSES * FEATS + 8 * piece
            out_ref[piece, CLASSES:, :] = total[start : start + 8, :]
        else:
            out_ref[piece, CLASSES:, :] = jnp.zeros((8, LANES), jnp.float32)


def moments_kernel(f_ref, q_ref, out_ref, low_ref, high_ref, total):
    count_x, count_y = q_ref.shape[0], q_ref.shape[1]
    per_x = count_y // GROUP
    total[...] = jnp.zeros_like(total)

    def step(c, carry):
        x, y = c // per_x, (c % per_x) * GROUP
        rows = [f_ref[x, y + g] for g in range(GROUP)]
        posts = [q_ref[x, y + g] for g in range(GROUP)]
        add_moments(rows, posts, total)
        face_of(jnp.concatenate(posts, axis=0), low_ref, high_ref, c)
        return carry

    lax.fori_loop(0, count_x * per_x, step, 0)
    pack_moments(total, out_ref)


def moments(f, q):
    faces = q.shape[0] * q.shape[1] * CLASSES
    return pl.pallas_call(
        moments_kernel,
        name="moments",
        out_shape=(
            jax.ShapeDtypeStruct((PIECES, PIECE_ROWS, LANES), jnp.float32),
            jax.ShapeDtypeStruct((1, faces), jnp.bfloat16),
            jax.ShapeDtypeStruct((1, faces), jnp.bfloat16),
        ),
        in_specs=[VMEM] * 2,
        out_specs=(VMEM,) * 3,
        scratch_shapes=[pltpu.VMEM((CLASSES * FEATS + CLASSES, LANES), jnp.float32)],
    )(f, q)


def sum_kernel(sizes, part_ref, out_ref, held_y, held_z, held_x, full, send, recv):
    me = {axis: lax.axis_index(axis) for axis in AXES}

    def partner(axis, d):
        return lax.rem(me[axis] + d, sizes[axis])

    barrier = pltpu.get_barrier_semaphore()
    for axis in AXES:
        for d in range(1, sizes[axis]):
            pl.semaphore_signal(
                barrier, inc=1, device_id={axis: partner(axis, d)}, device_id_type=MESH
            )
    pl.semaphore_wait(barrier, sum(sizes[axis] - 1 for axis in AXES))

    def exchange(stage, axis, source, held):
        copies = []
        for d in range(1, sizes[axis]):
            there = partner(axis, d)
            copies.append(
                pltpu.make_async_remote_copy(
                    src_ref=source(there),
                    dst_ref=held.at[me[axis]],
                    send_sem=send.at[stage, d],
                    recv_sem=recv.at[stage, d],
                    device_id={axis: there},
                    device_id_type=MESH,
                )
            )
        for copy in copies:
            copy.start()
        for copy in copies:
            copy.wait()

    def added(held, count):
        value = held[0]
        for i in range(1, count):
            value = value + held[i]
        return value

    y, z, x = me["gy"], me["gz"], me["gx"]
    group = PIECES // sizes["gy"]
    held_y[y] = part_ref[pl.ds(y * group, group)]
    exchange(0, "gy", lambda there: part_ref.at[pl.ds(there * group, group)], held_y)
    held_z[z] = added(held_y, sizes["gy"])
    exchange(1, "gz", lambda there: held_z.at[z], held_z)
    held_x[x] = added(held_z, sizes["gz"])
    exchange(2, "gx", lambda there: held_x.at[x], held_x)
    full[y] = added(held_x, sizes["gx"])
    exchange(3, "gy", lambda there: full.at[y], full)
    for i in range(sizes["gy"]):
        out_ref[pl.ds(i * group, group)] = full[i]


def summed(part):
    sizes = {axis: lax.axis_size(axis) for axis in AXES}
    most = max(sizes.values())
    block = (PIECES // sizes["gy"], PIECE_ROWS, LANES)
    return pl.pallas_call(
        functools.partial(sum_kernel, sizes),
        name="sum_over_devices",
        out_shape=jax.ShapeDtypeStruct(part.shape, jnp.float32),
        in_specs=[VMEM],
        out_specs=VMEM,
        scratch_shapes=[
            pltpu.VMEM((sizes["gy"],) + block, jnp.float32),
            pltpu.VMEM((sizes["gz"],) + block, jnp.float32),
            pltpu.VMEM((sizes["gx"],) + block, jnp.float32),
            pltpu.VMEM((sizes["gy"],) + block, jnp.float32),
            pltpu.SemaphoreType.DMA((4, most)),
            pltpu.SemaphoreType.DMA((4, most)),
        ],
        compiler_params=pltpu.CompilerParams(collective_id=0, has_side_effects=True),
    )(part)


def finish_kernel(sum_ref, matrix_ref, bias_ref, mean_ref):
    last = jnp.concatenate([sum_ref[0, CLASSES:, :], sum_ref[1, CLASSES:, :]], axis=0)
    counts = last[:, FEATS : FEATS + 1]
    mean = last[:, :FEATS] / counts
    mean_ref[...] = mean
    total_weight = jnp.sum(counts, axis=0, keepdims=True)
    lane = lax.broadcasted_iota(jnp.int32, (CLASSES, LANES), 1)
    small = lax.broadcasted_iota(jnp.int32, (CLASSES, FEATS), 1)
    rows_per = FEATS // PIECES
    rows = []
    for i in range(FEATS):
        start = (i % rows_per) * FEATS
        second = sum_ref[i // rows_per, :CLASSES, start : start + FEATS]
        spread = second / counts - mean[:, i : i + 1] * mean + jnp.where(small == i, ridge, 0.0)
        unit = jnp.where(small == i, 1.0, 0.0)
        shift = jnp.where(small == 0, mean[:, i : i + 1], 0.0)
        rows.append(jnp.concatenate([unit, shift, spread, jnp.zeros_like(spread)], axis=1))
    diagonal = jnp.ones((CLASSES, LANES), jnp.float32)
    for k in range(FEATS):
        pivot = jnp.sqrt(rows[k][:, 64 + k : 65 + k])
        diagonal = jnp.where(lane == k, pivot, diagonal)
        row = rows[k] * (1.0 / pivot)
        rows[k] = row
        for i in range(k + 1, FEATS):
            rows[i] = rows[i] - row[:, 64 + i : 65 + i] * row
    logdet = jnp.sum(jnp.log(diagonal), axis=1, keepdims=True)
    bias_ref[...] = jnp.broadcast_to(jnp.log(counts / total_weight) - logdet, (CLASSES, LANES))
    for g in range(FEATS):
        offset = -rows[g][:, FEATS : FEATS + 1]
        high = offset.astype(jnp.bfloat16).astype(jnp.float32)
        middle = (offset - high).astype(jnp.bfloat16).astype(jnp.float32)
        low = offset - high - middle
        tail = jnp.where(lane == 34, low, 0.0)
        tail = jnp.where(lane == 33, middle, tail)
        tail = jnp.where(lane == 32, high, tail)
        value = jnp.where(lane < FEATS, rows[g], tail)
        matrix_ref[g * CLASSES : (g + 1) * CLASSES, :] = value.astype(jnp.bfloat16)


def finish(total):
    return pl.pallas_call(
        finish_kernel,
        name="finish",
        out_shape=(
            jax.ShapeDtypeStruct((FEATS * CLASSES, LANES), jnp.bfloat16),
            jax.ShapeDtypeStruct((CLASSES, LANES), jnp.float32),
            jax.ShapeDtypeStruct((CLASSES, FEATS), jnp.float32),
        ),
        in_specs=[VMEM],
        out_specs=(VMEM,) * 3,
    )(total)


def fill_padded(padded, q_ref, xlo_ref, xhi_ref, ylo_ref, yhi_ref):
    count_x, count_y = q_ref.shape[0], q_ref.shape[1]
    padded[0, 1 : count_y + 1] = xlo_ref[...]
    padded[count_x + 1, 1 : count_y + 1] = xhi_ref[...]
    for x in range(count_x):
        padded[x + 1, 1 : count_y + 1] = q_ref[x]
        padded[x + 1, 0] = ylo_ref[x]
        padded[x + 1, count_y + 1] = yhi_ref[x]


def near_of(padded, zlo_ref, zhi_ref, x, y, c):
    flat = (GROUP * CLASSES, LANES)

    def block(dx, dy):
        return padded[x + 1 + dx, pl.ds(y + 1 + dy, GROUP)].reshape(flat)

    total = block(1, 0).astype(jnp.float32) + block(-1, 0).astype(jnp.float32)
    total = total + block(0, 1).astype(jnp.float32) + block(0, -1).astype(jnp.float32)
    a = lax.broadcasted_iota(jnp.int32, (LANES, LANES), 0)
    b = lax.broadcasted_iota(jnp.int32, (LANES, LANES), 1)
    beside = jnp.where((a == b + 1) | (a + 1 == b), 1.0, 0.0).astype(jnp.bfloat16)
    total = total + jnp.dot(block(0, 0), beside, preferred_element_type=jnp.float32)
    width = GROUP * CLASSES
    where = pl.ds(pl.multiple_of(c * width, width), width)
    side = lax.broadcasted_iota(jnp.int32, (8, width), 0)
    low = jnp.broadcast_to(zlo_ref[:, where].astype(jnp.float32), (8, width))
    high = jnp.broadcast_to(zhi_ref[:, where].astype(jnp.float32), (8, width))
    column = jnp.transpose(jnp.where(side == 0, low, high))
    lane = lax.broadcasted_iota(jnp.int32, flat, 1)
    edge = jnp.where(lane == LANES - 1, column[:, 1:2], 0.0)
    return total + jnp.where(lane == 0, column[:, 0:1], edge)


def update(scores, near):
    value = (scores + beta_coupling * near).reshape(GROUP, CLASSES, LANES)
    value = jnp.exp(value - jnp.max(value, axis=1, keepdims=True))
    value = value * (1.0 / jnp.sum(value, axis=1, keepdims=True))
    return value.astype(jnp.bfloat16)


def scores_of(f_ref, matrix_ref, bias_ref, x, y):
    bias = bias_ref[...]
    parts = []
    for g in range(0, GROUP, 2):
        pair = jnp.concatenate([f_ref[x, y + g], f_ref[x, y + g + 1]], axis=1)
        pair = augmented(pair)
        total = None
        for m in range(0, FEATS * CLASSES, 128):
            white = jnp.dot(
                matrix_ref[m : m + 128, :AUG], pair, preferred_element_type=jnp.float32
            )
            square = jnp.sum((white * white).reshape(128 // CLASSES, CLASSES, 2 * LANES), axis=0)
            total = square if total is None else total + square
        parts.append(bias - 0.5 * total[:, :LANES])
        parts.append(bias - 0.5 * total[:, LANES:])
    return jnp.concatenate(parts, axis=0)


def first_kernel(f_ref, m_ref, b_ref, q_ref, xlo, xhi, ylo, yhi, zlo, zhi,
                 out_ref, scores_ref, low_ref, high_ref, padded):
    count_x, count_y = q_ref.shape[0], q_ref.shape[1]
    per_x = count_y // GROUP
    fill_padded(padded, q_ref, xlo, xhi, ylo, yhi)

    def step(c, carry):
        x, y = c // per_x, (c % per_x) * GROUP
        scores = scores_of(f_ref, m_ref, b_ref, x, y)
        scores_ref[x, pl.ds(y, GROUP)] = scores.reshape(GROUP, CLASSES, LANES)
        q = update(scores, near_of(padded, zlo, zhi, x, y, c))
        out_ref[x, pl.ds(y, GROUP)] = q
        face_of(q.reshape(GROUP * CLASSES, LANES), low_ref, high_ref, c)
        return carry

    lax.fori_loop(0, count_x * per_x, step, 0)


def second_kernel(f_ref, scores_ref, q_ref, xlo, xhi, ylo, yhi, zlo, zhi,
                  out_ref, sum_ref, low_ref, high_ref, padded, total):
    count_x, count_y = q_ref.shape[0], q_ref.shape[1]
    per_x = count_y // GROUP
    fill_padded(padded, q_ref, xlo, xhi, ylo, yhi)
    total[...] = jnp.zeros_like(total)

    def step(c, carry):
        x, y = c // per_x, (c % per_x) * GROUP
        scores = scores_ref[x, pl.ds(y, GROUP)].reshape(GROUP * CLASSES, LANES)
        q = update(scores, near_of(padded, zlo, zhi, x, y, c))
        out_ref[x, pl.ds(y, GROUP)] = q
        rows = [f_ref[x, y + g] for g in range(GROUP)]
        add_moments(rows, [q[g] for g in range(GROUP)], total)
        face_of(q.reshape(GROUP * CLASSES, LANES), low_ref, high_ref, c)
        return carry

    lax.fori_loop(0, count_x * per_x, step, 0)
    pack_moments(total, sum_ref)


def last_kernel(f_ref, m_ref, b_ref, q_ref, xlo, xhi, ylo, yhi, zlo, zhi, out_ref, padded):
    count_x, count_y = q_ref.shape[0], q_ref.shape[1]
    per_x = count_y // GROUP
    fill_padded(padded, q_ref, xlo, xhi, ylo, yhi)

    def step(c, carry):
        x, y = c // per_x, (c % per_x) * GROUP
        scores = scores_of(f_ref, m_ref, b_ref, x, y)
        out_ref[x, pl.ds(y, GROUP)] = update(scores, near_of(padded, zlo, zhi, x, y, c))
        return carry

    lax.fori_loop(0, count_x * per_x, step, 0)


def sweep_call(kernel, name, operands, q, out_shape, scratch=()):
    count_x, count_y = q.shape[0], q.shape[1]
    padded = pltpu.VMEM((count_x + 2, count_y + 2, CLASSES, LANES), jnp.bfloat16)
    return pl.pallas_call(
        kernel,
        name=name,
        out_shape=out_shape,
        in_specs=[VMEM] * len(operands),
        out_specs=jax.tree.map(lambda _: VMEM, out_shape),
        scratch_shapes=[padded] + list(scratch),
    )(*operands)


def halo_of(q, low, high):
    faces = {"gx": (q[0], q[-1]), "gy": (q[:, 0], q[:, -1]), "gz": (low, high)}
    got = []
    for axis, (first, last) in faces.items():
        count = lax.axis_size(axis)
        up = [(i, i + 1) for i in range(count - 1)]
        down = [(j, i) for i, j in up]
        got.append(lax.ppermute(last, axis, up))
        got.append(lax.ppermute(first, axis, down))
    return got


def local(features, posteriors):
    f = features.transpose(1, 2, 0, 3)
    q = posteriors.transpose(1, 2, 0, 3)
    face = jax.ShapeDtypeStruct((1, q.shape[0] * q.shape[1] * CLASSES), jnp.bfloat16)
    state = jax.ShapeDtypeStruct(q.shape, jnp.bfloat16)
    scores_shape = jax.ShapeDtypeStruct(q.shape, jnp.float32)
    sums = jax.ShapeDtypeStruct((PIECES, PIECE_ROWS, LANES), jnp.float32)
    total = pltpu.VMEM((CLASSES * FEATS + CLASSES, LANES), jnp.float32)

    part, low, high = moments(f, q)
    halo = halo_of(q, low, high)
    matrix, bias, _ = finish(summed(part))
    q, scores, low, high = sweep_call(
        first_kernel, "first_sweep", [f, matrix, bias, q] + halo, q,
        (state, scores_shape, face, face))
    halo = halo_of(q, low, high)
    q, part, low, high = sweep_call(
        second_kernel, "second_sweep", [f, scores, q] + halo, q,
        (state, sums, face, face), [total])
    halo = halo_of(q, low, high)
    matrix, bias, mean = finish(summed(part))
    q = sweep_call(last_kernel, "last_update", [f, matrix, bias, q] + halo, q, state)
    return (q.transpose(2, 0, 1, 3), mean)


def solution(mesh):
    placed = P(None, "gx", "gy", "gz")
    return jax.shard_map(
        local,
        mesh=mesh,
        in_specs=(placed, placed),
        out_specs=(placed, P()),
        check_vma=False,
    )
```

```python
import functools

import jax
import jax.numpy as jnp
from jax import lax
from jax.experimental import pallas as pl
from jax.experimental.pallas import tpu as pltpu
from jax.sharding import PartitionSpec as P

SWEEPS = 2
FEATS = 32
CLASSES = 16
LANES = 128
GROUP = 8
PIECES = 16
PIECE_ROWS = 9
HALVES = 2
AUG = 48

beta_coupling = 1.0
ridge = 0.1

AXES = ("gx", "gy", "gz")
MESH = pl.DeviceIdType.MESH
VMEM = pl.BlockSpec(memory_space=pltpu.VMEM)
NT = (((1,), (1,)), ((), ()))


def augmented(rows):
    count = rows.shape[1]
    index = lax.broadcasted_iota(jnp.int32, (AUG - FEATS, count), 0)
    extra = jnp.where(index < 3, 1.0, 0.0).astype(jnp.bfloat16)
    return jnp.concatenate([rows, extra], axis=0)


def face_of(q_rows, low_ref, high_ref, step):
    side = lax.broadcasted_iota(jnp.int32, (16, LANES), 0)
    lane = lax.broadcasted_iota(jnp.int32, (16, LANES), 1)
    pick = ((side == 0) & (lane == 0)) | ((side == 1) & (lane == LANES - 1))
    pick = jnp.where(pick, 1.0, 0.0).astype(jnp.bfloat16)
    faces = lax.dot_general(pick, q_rows, NT, preferred_element_type=jnp.float32)
    width = GROUP * CLASSES
    where = pl.ds(pl.multiple_of(step * width, width), width)
    low_ref[:, where] = faces[0:1].astype(jnp.bfloat16)
    high_ref[:, where] = faces[1:2].astype(jnp.bfloat16)


def add_moments(rows, posts, total):
    weighted = []
    for row, post in zip(rows, posts):
        parts = [post[k : k + 1, :] * row for k in range(CLASSES)] + [post]
        weighted.append(jnp.concatenate(parts, axis=0))
    left = jnp.concatenate(weighted, axis=1)
    right = augmented(jnp.concatenate(rows, axis=1))
    total[:, :AUG] += lax.dot_general(left, right, NT, preferred_element_type=jnp.float32)


def pack_moments(total, out_ref):
    rows_per = LANES // FEATS
    for part in range(FEATS // rows_per):
        blocks = []
        for r in range(rows_per):
            row = part * rows_per + r
            blocks.append(total[pl.ds(row, CLASSES, stride=FEATS), :][:, :FEATS])
        block = jnp.concatenate(blocks, axis=1)
        out_ref[2 * part, :8, :] = block[:8]
        out_ref[2 * part + 1, :8, :] = block[8:]
    for k in range(CLASSES):
        start = CLASSES * FEATS + k
        out_ref[k, 8:9, :] = total[start : start + 1, :]


def moments_kernel(f_ref, q_ref, out_ref, low_ref, high_ref, total):
    count_x, count_y = q_ref.shape[0], q_ref.shape[1]
    per_x = count_y // GROUP
    total[...] = jnp.zeros_like(total)

    def step(c, carry):
        x, y = c // per_x, (c % per_x) * GROUP
        rows = [f_ref[x, y + g] for g in range(GROUP)]
        posts = [q_ref[x, y + g] for g in range(GROUP)]
        add_moments(rows, posts, total)
        face_of(jnp.concatenate(posts, axis=0), low_ref, high_ref, c)
        return carry

    lax.fori_loop(0, count_x * per_x, step, 0)
    pack_moments(total, out_ref)


def moments(f, q):
    faces = q.shape[0] * q.shape[1] * CLASSES
    return pl.pallas_call(
        moments_kernel,
        name="moments",
        out_shape=(
            jax.ShapeDtypeStruct((PIECES, PIECE_ROWS, LANES), jnp.float32),
            jax.ShapeDtypeStruct((1, faces), jnp.bfloat16),
            jax.ShapeDtypeStruct((1, faces), jnp.bfloat16),
        ),
        in_specs=[VMEM] * 2,
        out_specs=(VMEM,) * 3,
        scratch_shapes=[pltpu.VMEM((CLASSES * FEATS + CLASSES, LANES), jnp.float32)],
    )(f, q)


def places(sizes):
    gx, gy, gz = (lax.axis_index(axis) for axis in AXES)
    depth = sizes["gz"] // HALVES
    half, y = lax.div(gz, depth), lax.rem(gz, depth)
    ring, plane = gy * HALVES + half, gx * depth + y
    rings, planes = sizes["gy"] * HALVES, sizes["gx"] * depth

    def in_ring(d):
        there = lax.rem(ring + d, rings)
        return there, {
            "gy": lax.div(there, HALVES),
            "gz": lax.rem(there, HALVES) * depth + y,
        }

    def in_plane(d):
        there = lax.rem(plane + d, planes)
        return there, {"gx": lax.div(there, depth), "gz": half * depth + lax.rem(there, depth)}

    return (ring, rings, in_ring), (plane, planes, in_plane)


def beside(sizes, axis, d):
    return {axis: lax.rem(lax.axis_index(axis) + d + sizes[axis], sizes[axis])}


def meet(devices):
    barrier = pltpu.get_barrier_semaphore()
    for device in devices:
        pl.semaphore_signal(barrier, inc=1, device_id=device, device_id_type=MESH)
    pl.semaphore_wait(barrier, len(devices))


def remote(source, target, send, recv, device):
    copy = pltpu.make_async_remote_copy(
        src_ref=source, dst_ref=target, send_sem=send, recv_sem=recv,
        device_id=device, device_id_type=MESH,
    )
    copy.start()
    return copy


def start_halo(sizes, q_ref, low_ref, high_ref, halo, send, recv):
    last_x, last_y = q_ref.shape[0] - 1, q_ref.shape[1] - 1
    faces = {
        "gx": (q_ref.at[0], q_ref.at[last_x]),
        "gy": (q_ref.at[:, 0], q_ref.at[:, last_y]),
        "gz": (low_ref, high_ref),
    }
    copies = []
    for n, (axis, (first, last)) in enumerate(faces.items()):
        up, down = 2 * n, 2 * n + 1
        copies.append(
            remote(last, halo[up], send.at[up], recv.at[up], beside(sizes, axis, 1))
        )
        copies.append(
            remote(first, halo[down], send.at[down], recv.at[down], beside(sizes, axis, -1))
        )
    return copies


def end_halo(sizes, copies, halo):
    for copy in copies:
        copy.wait()
    for n, axis in enumerate(AXES):
        for ref, edge in ((halo[2 * n], 0), (halo[2 * n + 1], sizes[axis] - 1)):

            @pl.when(lax.axis_index(axis) == edge)
            def _(ref=ref):
                ref[...] = jnp.zeros_like(ref)


def halo_kernel(sizes, q_ref, low_ref, high_ref, *rest):
    halo, (send, recv) = rest[:6], rest[6:]
    meet([beside(sizes, axis, d) for axis in AXES for d in (1, -1)])
    end_halo(sizes, start_halo(sizes, q_ref, low_ref, high_ref, halo, send, recv), halo)


def sum_kernel(sizes, part_ref, q_ref, low_ref, high_ref, out_ref, *rest):
    halo, (held, planar, full, send, recv, halo_send, halo_recv) = rest[:6], rest[6:]
    (ring, rings, in_ring), (plane, planes, in_plane) = places(sizes)
    devices = [in_ring(d)[1] for d in range(1, rings)]
    devices += [in_plane(d)[1] for d in range(1, planes)]
    meet(devices + [beside(sizes, "gz", 1), beside(sizes, "gz", -1)])
    group = PIECES // rings

    def added(ref, count):
        value = ref[0]
        for i in range(1, count):
            value = value + ref[i]
        return value

    held[ring] = part_ref[pl.ds(ring * group, group)]
    copies = []
    for d in range(1, rings):
        there, device = in_ring(d)
        source = part_ref.at[pl.ds(there * group, group)]
        copies.append(remote(source, held.at[ring], send.at[0, d], recv.at[0, d], device))
    halo_copies = start_halo(sizes, q_ref, low_ref, high_ref, halo, halo_send, halo_recv)
    for copy in copies:
        copy.wait()
    planar[plane] = added(held, rings)
    copies = []
    for d in range(1, planes):
        _, device = in_plane(d)
        place = planar.at[plane]
        copies.append(remote(place, place, send.at[1, d], recv.at[1, d], device))
    for copy in copies:
        copy.wait()
    full[ring] = added(planar, planes)
    copies = []
    for d in range(1, rings):
        _, device = in_ring(d)
        place = full.at[ring]
        copies.append(remote(place, place, send.at[2, d], recv.at[2, d], device))
    for copy in copies:
        copy.wait()
    for i in range(rings):
        out_ref[i * group : (i + 1) * group] = full[i]
    end_halo(sizes, halo_copies, halo)


def halo_shapes(q, low):
    plane_x = jax.ShapeDtypeStruct(q.shape[1:], q.dtype)
    plane_y = jax.ShapeDtypeStruct((q.shape[0],) + q.shape[2:], q.dtype)
    plane_z = jax.ShapeDtypeStruct(low.shape, low.dtype)
    return (plane_x, plane_x, plane_y, plane_y, plane_z, plane_z)


def halo_of(q, low, high):
    sizes = {axis: lax.axis_size(axis) for axis in AXES}
    return pl.pallas_call(
        functools.partial(halo_kernel, sizes),
        name="halo",
        out_shape=halo_shapes(q, low),
        in_specs=[VMEM] * 3,
        out_specs=(VMEM,) * 6,
        scratch_shapes=[pltpu.SemaphoreType.DMA((6,)), pltpu.SemaphoreType.DMA((6,))],
        compiler_params=pltpu.CompilerParams(collective_id=1, has_side_effects=True),
    )(q, low, high)


def summed(part, q, low, high):
    sizes = {axis: lax.axis_size(axis) for axis in AXES}
    rings, planes = sizes["gy"] * HALVES, sizes["gx"] * (sizes["gz"] // HALVES)
    block = (PIECES // rings, PIECE_ROWS, LANES)
    most = max(rings, planes)
    total, *halo = pl.pallas_call(
        functools.partial(sum_kernel, sizes),
        name="sum_and_halo",
        out_shape=(jax.ShapeDtypeStruct(part.shape, jnp.float32),) + halo_shapes(q, low),
        in_specs=[VMEM] * 4,
        out_specs=(VMEM,) * 7,
        scratch_shapes=[
            pltpu.VMEM((rings,) + block, jnp.float32),
            pltpu.VMEM((planes,) + block, jnp.float32),
            pltpu.VMEM((rings,) + block, jnp.float32),
            pltpu.SemaphoreType.DMA((3, most)),
            pltpu.SemaphoreType.DMA((3, most)),
            pltpu.SemaphoreType.DMA((6,)),
            pltpu.SemaphoreType.DMA((6,)),
        ],
        compiler_params=pltpu.CompilerParams(collective_id=0, has_side_effects=True),
    )(part, q, low, high)
    return total, halo


def finish_kernel(sum_ref, matrix_ref, bias_ref, mean_ref):
    last = jnp.concatenate([sum_ref[k, 8:9, :] for k in range(CLASSES)], axis=0)
    counts = last[:, FEATS : FEATS + 1]
    mean = last[:, :FEATS] / counts
    mean_ref[...] = mean
    total_weight = jnp.sum(counts, axis=0, keepdims=True)
    lane = lax.broadcasted_iota(jnp.int32, (CLASSES, LANES), 1)
    small = lax.broadcasted_iota(jnp.int32, (CLASSES, FEATS), 1)
    rows_per = LANES // FEATS
    rows = []
    for i in range(FEATS):
        start = (i % rows_per) * FEATS
        part = 2 * (i // rows_per)
        second = jnp.concatenate([sum_ref[part, :8, :], sum_ref[part + 1, :8, :]], axis=0)
        second = second[:, start : start + FEATS]
        spread = second / counts - mean[:, i : i + 1] * mean + jnp.where(small == i, ridge, 0.0)
        unit = jnp.where(small == i, 1.0, 0.0)
        shift = jnp.where(small == 0, mean[:, i : i + 1], 0.0)
        rows.append(jnp.concatenate([unit, shift, spread, jnp.zeros_like(spread)], axis=1))
    diagonal = jnp.ones((CLASSES, LANES), jnp.float32)
    for k in range(FEATS):
        pivot = jnp.sqrt(rows[k][:, 64 + k : 65 + k])
        diagonal = jnp.where(lane == k, pivot, diagonal)
        row = rows[k] * (1.0 / pivot)
        rows[k] = row
        for i in range(k + 1, FEATS):
            rows[i] = rows[i] - row[:, 64 + i : 65 + i] * row
    logdet = jnp.sum(jnp.log(diagonal), axis=1, keepdims=True)
    bias_ref[...] = jnp.broadcast_to(jnp.log(counts / total_weight) - logdet, (CLASSES, LANES))
    for g in range(FEATS):
        offset = -rows[g][:, FEATS : FEATS + 1]
        high = offset.astype(jnp.bfloat16).astype(jnp.float32)
        middle = (offset - high).astype(jnp.bfloat16).astype(jnp.float32)
        low = offset - high - middle
        tail = jnp.where(lane == 34, low, 0.0)
        tail = jnp.where(lane == 33, middle, tail)
        tail = jnp.where(lane == 32, high, tail)
        value = jnp.where(lane < FEATS, rows[g], tail)
        matrix_ref[g * CLASSES : (g + 1) * CLASSES, :] = value.astype(jnp.bfloat16)


def finish(total):
    return pl.pallas_call(
        finish_kernel,
        name="finish",
        out_shape=(
            jax.ShapeDtypeStruct((FEATS * CLASSES, LANES), jnp.bfloat16),
            jax.ShapeDtypeStruct((CLASSES, LANES), jnp.float32),
            jax.ShapeDtypeStruct((CLASSES, FEATS), jnp.float32),
        ),
        in_specs=[VMEM],
        out_specs=(VMEM,) * 3,
    )(total)


def fill_padded(padded, q_ref, xlo_ref, xhi_ref, ylo_ref, yhi_ref):
    count_x, count_y = q_ref.shape[0], q_ref.shape[1]
    padded[0, 1 : count_y + 1] = xlo_ref[...]
    padded[count_x + 1, 1 : count_y + 1] = xhi_ref[...]
    for x in range(count_x):
        padded[x + 1, 1 : count_y + 1] = q_ref[x]
        padded[x + 1, 0] = ylo_ref[x]
        padded[x + 1, count_y + 1] = yhi_ref[x]


def near_of(padded, zlo_ref, zhi_ref, x, y, c):
    flat = (GROUP * CLASSES, LANES)

    def block(dx, dy):
        return padded[x + 1 + dx, pl.ds(y + 1 + dy, GROUP)].reshape(flat)

    total = block(1, 0).astype(jnp.float32) + block(-1, 0).astype(jnp.float32)
    total = total + block(0, 1).astype(jnp.float32) + block(0, -1).astype(jnp.float32)
    a = lax.broadcasted_iota(jnp.int32, (LANES, LANES), 0)
    b = lax.broadcasted_iota(jnp.int32, (LANES, LANES), 1)
    shift = jnp.where((a == b + 1) | (a + 1 == b), 1.0, 0.0).astype(jnp.bfloat16)
    total = total + jnp.dot(block(0, 0), shift, preferred_element_type=jnp.float32)
    width = GROUP * CLASSES
    where = pl.ds(pl.multiple_of(c * width, width), width)
    side = lax.broadcasted_iota(jnp.int32, (8, width), 0)
    low = jnp.broadcast_to(zlo_ref[:, where].astype(jnp.float32), (8, width))
    high = jnp.broadcast_to(zhi_ref[:, where].astype(jnp.float32), (8, width))
    column = jnp.transpose(jnp.where(side == 0, low, high))
    lane = lax.broadcasted_iota(jnp.int32, flat, 1)
    edge = jnp.where(lane == LANES - 1, column[:, 1:2], 0.0)
    return total + jnp.where(lane == 0, column[:, 0:1], edge)


def update(scores, near):
    value = (scores + beta_coupling * near).reshape(GROUP, CLASSES, LANES)
    value = jnp.exp(value - jnp.max(value, axis=1, keepdims=True))
    value = value * (1.0 / jnp.sum(value, axis=1, keepdims=True))
    return value.astype(jnp.bfloat16)


def scores_of(f_ref, matrix_ref, bias_ref, x, y):
    bias = bias_ref[...]
    parts = []
    for g in range(0, GROUP, 2):
        pair = jnp.concatenate([f_ref[x, y + g], f_ref[x, y + g + 1]], axis=1)
        pair = augmented(pair)
        total = None
        for m in range(0, FEATS * CLASSES, 128):
            white = jnp.dot(
                matrix_ref[m : m + 128, :AUG], pair, preferred_element_type=jnp.float32
            )
            square = jnp.sum((white * white).reshape(128 // CLASSES, CLASSES, 2 * LANES), axis=0)
            total = square if total is None else total + square
        parts.append(bias - 0.5 * total[:, :LANES])
        parts.append(bias - 0.5 * total[:, LANES:])
    return jnp.concatenate(parts, axis=0)


def first_kernel(f_ref, m_ref, b_ref, q_ref, xlo, xhi, ylo, yhi, zlo, zhi,
                 out_ref, scores_ref, low_ref, high_ref, padded):
    count_x, count_y = q_ref.shape[0], q_ref.shape[1]
    per_x = count_y // GROUP
    fill_padded(padded, q_ref, xlo, xhi, ylo, yhi)

    def step(c, carry):
        x, y = c // per_x, (c % per_x) * GROUP
        scores = scores_of(f_ref, m_ref, b_ref, x, y)
        scores_ref[x, pl.ds(y, GROUP)] = scores.reshape(GROUP, CLASSES, LANES)
        q = update(scores, near_of(padded, zlo, zhi, x, y, c))
        out_ref[x, pl.ds(y, GROUP)] = q
        face_of(q.reshape(GROUP * CLASSES, LANES), low_ref, high_ref, c)
        return carry

    lax.fori_loop(0, count_x * per_x, step, 0)


def second_kernel(f_ref, scores_ref, q_ref, xlo, xhi, ylo, yhi, zlo, zhi,
                  out_ref, sum_ref, low_ref, high_ref, padded, total):
    count_x, count_y = q_ref.shape[0], q_ref.shape[1]
    per_x = count_y // GROUP
    fill_padded(padded, q_ref, xlo, xhi, ylo, yhi)
    total[...] = jnp.zeros_like(total)

    def step(c, carry):
        x, y = c // per_x, (c % per_x) * GROUP
        scores = scores_ref[x, pl.ds(y, GROUP)].reshape(GROUP * CLASSES, LANES)
        q = update(scores, near_of(padded, zlo, zhi, x, y, c))
        out_ref[x, pl.ds(y, GROUP)] = q
        rows = [f_ref[x, y + g] for g in range(GROUP)]
        add_moments(rows, [q[g] for g in range(GROUP)], total)
        face_of(q.reshape(GROUP * CLASSES, LANES), low_ref, high_ref, c)
        return carry

    lax.fori_loop(0, count_x * per_x, step, 0)
    pack_moments(total, sum_ref)


def last_kernel(f_ref, m_ref, b_ref, q_ref, xlo, xhi, ylo, yhi, zlo, zhi, out_ref, padded):
    count_x, count_y = q_ref.shape[0], q_ref.shape[1]
    per_x = count_y // GROUP
    fill_padded(padded, q_ref, xlo, xhi, ylo, yhi)

    def step(c, carry):
        x, y = c // per_x, (c % per_x) * GROUP
        scores = scores_of(f_ref, m_ref, b_ref, x, y)
        out_ref[x, pl.ds(y, GROUP)] = update(scores, near_of(padded, zlo, zhi, x, y, c))
        return carry

    lax.fori_loop(0, count_x * per_x, step, 0)


def sweep_call(kernel, name, operands, q, out_shape, scratch=()):
    count_x, count_y = q.shape[0], q.shape[1]
    padded = pltpu.VMEM((count_x + 2, count_y + 2, CLASSES, LANES), jnp.bfloat16)
    return pl.pallas_call(
        kernel,
        name=name,
        out_shape=out_shape,
        in_specs=[VMEM] * len(operands),
        out_specs=jax.tree.map(lambda _: VMEM, out_shape),
        scratch_shapes=[padded] + list(scratch),
    )(*operands)


def local(features, posteriors):
    f = features.transpose(1, 2, 0, 3)
    q = posteriors.transpose(1, 2, 0, 3)
    face = jax.ShapeDtypeStruct((1, q.shape[0] * q.shape[1] * CLASSES), jnp.bfloat16)
    state = jax.ShapeDtypeStruct(q.shape, jnp.bfloat16)
    scores_shape = jax.ShapeDtypeStruct(q.shape, jnp.float32)
    sums = jax.ShapeDtypeStruct((PIECES, PIECE_ROWS, LANES), jnp.float32)
    total = pltpu.VMEM((CLASSES * FEATS + CLASSES, LANES), jnp.float32)

    part, low, high = moments(f, q)
    total_sum, halo = summed(part, q, low, high)
    matrix, bias, _ = finish(total_sum)
    q, scores, low, high = sweep_call(
        first_kernel, "first_sweep", [f, matrix, bias, q, *halo], q,
        (state, scores_shape, face, face))
    halo = halo_of(q, low, high)
    q, part, low, high = sweep_call(
        second_kernel, "second_sweep", [f, scores, q, *halo], q,
        (state, sums, face, face), [total])
    total_sum, halo = summed(part, q, low, high)
    matrix, bias, mean = finish(total_sum)
    q = sweep_call(last_kernel, "last_update", [f, matrix, bias, q, *halo], q, state)
    return (q.transpose(2, 0, 1, 3), mean)


def solution(mesh):
    placed = P(None, "gx", "gy", "gz")
    return jax.shard_map(
        local,
        mesh=mesh,
        in_specs=(placed, placed),
        out_specs=(placed, P()),
        check_vma=False,
    )
```

```python
import functools

import jax
import jax.numpy as jnp
from jax import lax
from jax.experimental import pallas as pl
from jax.experimental.pallas import tpu as pltpu
from jax.sharding import PartitionSpec as P

SWEEPS = 2
FEATS = 32
CLASSES = 16
LANES = 128
GROUP = 8
PIECES = 16
PIECE_ROWS = 9
HALVES = 2
AUG = 48

UNROLL = 8
LIMIT = 20 << 20
MATRIX_ROWS = 128

beta_coupling = 1.0
ridge = 0.1

AXES = ("gx", "gy", "gz")
MESH = pl.DeviceIdType.MESH
VMEM = pl.BlockSpec(memory_space=pltpu.VMEM)
NT = (((1,), (1,)), ((), ()))


def augmented(rows):
    count = rows.shape[1]
    index = lax.broadcasted_iota(jnp.int32, (AUG - FEATS, count), 0)
    extra = jnp.where(index < 3, 1.0, 0.0).astype(jnp.bfloat16)
    return jnp.concatenate([rows, extra], axis=0)


def face_of(q_rows, low_ref, high_ref, step):
    side = lax.broadcasted_iota(jnp.int32, (16, LANES), 0)
    lane = lax.broadcasted_iota(jnp.int32, (16, LANES), 1)
    pick = ((side == 0) & (lane == 0)) | ((side == 1) & (lane == LANES - 1))
    pick = jnp.where(pick, 1.0, 0.0).astype(jnp.bfloat16)
    faces = lax.dot_general(pick, q_rows, NT, preferred_element_type=jnp.float32)
    width = GROUP * CLASSES
    where = pl.ds(pl.multiple_of(step * width, width), width)
    low_ref[:, where] = faces[0:1].astype(jnp.bfloat16)
    high_ref[:, where] = faces[1:2].astype(jnp.bfloat16)


def add_moments(rows, posts, total):
    weighted = []
    for row, post in zip(rows, posts):
        parts = [post[k : k + 1, :] * row for k in range(CLASSES)] + [post]
        weighted.append(jnp.concatenate(parts, axis=0))
    left = jnp.concatenate(weighted, axis=1)
    right = augmented(jnp.concatenate(rows, axis=1))
    total[:, :AUG] += lax.dot_general(left, right, NT, preferred_element_type=jnp.float32)


def pack_moments(total, out_ref):
    rows_per = LANES // FEATS
    for part in range(FEATS // rows_per):
        blocks = []
        for r in range(rows_per):
            row = part * rows_per + r
            blocks.append(total[pl.ds(row, CLASSES, stride=FEATS), :][:, :FEATS])
        block = jnp.concatenate(blocks, axis=1)
        out_ref[2 * part, :8, :] = block[:8]
        out_ref[2 * part + 1, :8, :] = block[8:]
    for k in range(CLASSES):
        start = CLASSES * FEATS + k
        out_ref[k, 8:9, :] = total[start : start + 1, :]


def moments_kernel(f_ref, q_ref, out_ref, low_ref, high_ref, total):
    count_x, count_y = q_ref.shape[0], q_ref.shape[1]
    per_x = count_y // GROUP
    total[...] = jnp.zeros_like(total)

    def step(c, carry):
        x, y = c // per_x, (c % per_x) * GROUP
        rows = [f_ref[x, y + g] for g in range(GROUP)]
        posts = [q_ref[x, y + g] for g in range(GROUP)]
        add_moments(rows, posts, total)
        face_of(jnp.concatenate(posts, axis=0), low_ref, high_ref, c)
        return carry

    lax.fori_loop(0, count_x * per_x, step, 0, unroll=UNROLL)
    pack_moments(total, out_ref)


def moments(f, q):
    faces = q.shape[0] * q.shape[1] * CLASSES
    return pl.pallas_call(
        moments_kernel,
        name="moments",
        out_shape=(
            jax.ShapeDtypeStruct((PIECES, PIECE_ROWS, LANES), jnp.float32),
            jax.ShapeDtypeStruct((1, faces), jnp.bfloat16),
            jax.ShapeDtypeStruct((1, faces), jnp.bfloat16),
        ),
        in_specs=[VMEM] * 2,
        out_specs=(VMEM,) * 3,
        compiler_params=pltpu.CompilerParams(vmem_limit_bytes=LIMIT),
        scratch_shapes=[pltpu.VMEM((CLASSES * FEATS + CLASSES, LANES), jnp.float32)],
    )(f, q)


def places(sizes):
    gx, gy, gz = (lax.axis_index(axis) for axis in AXES)
    depth = sizes["gz"] // HALVES
    half, y = lax.div(gz, depth), lax.rem(gz, depth)
    ring, plane = gy * HALVES + half, gx * depth + y
    rings, planes = sizes["gy"] * HALVES, sizes["gx"] * depth

    def in_ring(d):
        there = lax.rem(ring + d, rings)
        return there, {
            "gy": lax.div(there, HALVES),
            "gz": lax.rem(there, HALVES) * depth + y,
        }

    def in_plane(d):
        there = lax.rem(plane + d, planes)
        return there, {"gx": lax.div(there, depth), "gz": half * depth + lax.rem(there, depth)}

    return (ring, rings, in_ring), (plane, planes, in_plane)


def beside(sizes, axis, d):
    return {axis: lax.rem(lax.axis_index(axis) + d + sizes[axis], sizes[axis])}


def meet(devices):
    barrier = pltpu.get_barrier_semaphore()
    for device in devices:
        pl.semaphore_signal(barrier, inc=1, device_id=device, device_id_type=MESH)
    pl.semaphore_wait(barrier, len(devices))


def remote(source, target, send, recv, device):
    copy = pltpu.make_async_remote_copy(
        src_ref=source, dst_ref=target, send_sem=send, recv_sem=recv,
        device_id=device, device_id_type=MESH,
    )
    copy.start()
    return copy


def start_halo(sizes, q_ref, low_ref, high_ref, halo, send, recv):
    last_x, last_y = q_ref.shape[0] - 1, q_ref.shape[1] - 1
    faces = {
        "gx": (q_ref.at[0], q_ref.at[last_x]),
        "gy": (q_ref.at[:, 0], q_ref.at[:, last_y]),
        "gz": (low_ref, high_ref),
    }
    copies = []
    for n, (axis, (first, last)) in enumerate(faces.items()):
        up, down = 2 * n, 2 * n + 1
        copies.append(
            remote(last, halo[up], send.at[up], recv.at[up], beside(sizes, axis, 1))
        )
        copies.append(
            remote(first, halo[down], send.at[down], recv.at[down], beside(sizes, axis, -1))
        )
    return copies


def end_halo(sizes, copies, halo):
    for copy in copies:
        copy.wait()
    for n, axis in enumerate(AXES):
        for ref, edge in ((halo[2 * n], 0), (halo[2 * n + 1], sizes[axis] - 1)):

            @pl.when(lax.axis_index(axis) == edge)
            def _(ref=ref):
                ref[...] = jnp.zeros_like(ref)


def halo_kernel(sizes, q_ref, low_ref, high_ref, *rest):
    halo, (send, recv) = rest[:6], rest[6:]
    meet([beside(sizes, axis, d) for axis in AXES for d in (1, -1)])
    end_halo(sizes, start_halo(sizes, q_ref, low_ref, high_ref, halo, send, recv), halo)


def sum_kernel(sizes, part_ref, q_ref, low_ref, high_ref, out_ref, *rest):
    halo, (held, planar, full, send, recv, halo_send, halo_recv) = rest[:6], rest[6:]
    (ring, rings, in_ring), (plane, planes, in_plane) = places(sizes)
    devices = [in_ring(d)[1] for d in range(1, rings)]
    devices += [in_plane(d)[1] for d in range(1, planes)]
    meet(devices + [beside(sizes, "gz", 1), beside(sizes, "gz", -1)])
    group = PIECES // rings

    def added(ref, count):
        value = ref[0]
        for i in range(1, count):
            value = value + ref[i]
        return value

    held[ring] = part_ref[pl.ds(ring * group, group)]
    copies = []
    for d in range(1, rings):
        there, device = in_ring(d)
        source = part_ref.at[pl.ds(there * group, group)]
        copies.append(remote(source, held.at[ring], send.at[0, d], recv.at[0, d], device))
    halo_copies = start_halo(sizes, q_ref, low_ref, high_ref, halo, halo_send, halo_recv)
    for copy in copies:
        copy.wait()
    planar[plane] = added(held, rings)
    copies = []
    for d in range(1, planes):
        _, device = in_plane(d)
        place = planar.at[plane]
        copies.append(remote(place, place, send.at[1, d], recv.at[1, d], device))
    for copy in copies:
        copy.wait()
    full[ring] = added(planar, planes)
    copies = []
    for d in range(1, rings):
        _, device = in_ring(d)
        place = full.at[ring]
        copies.append(remote(place, place, send.at[2, d], recv.at[2, d], device))
    for copy in copies:
        copy.wait()
    for i in range(rings):
        out_ref[i * group : (i + 1) * group] = full[i]
    end_halo(sizes, halo_copies, halo)


def halo_shapes(q, low):
    plane_x = jax.ShapeDtypeStruct(q.shape[1:], q.dtype)
    plane_y = jax.ShapeDtypeStruct((q.shape[0],) + q.shape[2:], q.dtype)
    plane_z = jax.ShapeDtypeStruct(low.shape, low.dtype)
    return (plane_x, plane_x, plane_y, plane_y, plane_z, plane_z)


def halo_of(q, low, high):
    sizes = {axis: lax.axis_size(axis) for axis in AXES}
    return pl.pallas_call(
        functools.partial(halo_kernel, sizes),
        name="halo",
        out_shape=halo_shapes(q, low),
        in_specs=[VMEM] * 3,
        out_specs=(VMEM,) * 6,
        scratch_shapes=[pltpu.SemaphoreType.DMA((6,)), pltpu.SemaphoreType.DMA((6,))],
        compiler_params=pltpu.CompilerParams(collective_id=1, vmem_limit_bytes=LIMIT, has_side_effects=True),
    )(q, low, high)


def summed(part, q, low, high):
    sizes = {axis: lax.axis_size(axis) for axis in AXES}
    rings, planes = sizes["gy"] * HALVES, sizes["gx"] * (sizes["gz"] // HALVES)
    block = (PIECES // rings, PIECE_ROWS, LANES)
    most = max(rings, planes)
    total, *halo = pl.pallas_call(
        functools.partial(sum_kernel, sizes),
        name="sum_and_halo",
        out_shape=(jax.ShapeDtypeStruct(part.shape, jnp.float32),) + halo_shapes(q, low),
        in_specs=[VMEM] * 4,
        out_specs=(VMEM,) * 7,
        scratch_shapes=[
            pltpu.VMEM((rings,) + block, jnp.float32),
            pltpu.VMEM((planes,) + block, jnp.float32),
            pltpu.VMEM((rings,) + block, jnp.float32),
            pltpu.SemaphoreType.DMA((3, most)),
            pltpu.SemaphoreType.DMA((3, most)),
            pltpu.SemaphoreType.DMA((6,)),
            pltpu.SemaphoreType.DMA((6,)),
        ],
        compiler_params=pltpu.CompilerParams(collective_id=0, vmem_limit_bytes=LIMIT, has_side_effects=True),
    )(part, q, low, high)
    return total, halo


def finish_kernel(sum_ref, matrix_ref, bias_ref, mean_ref):
    last = jnp.concatenate([sum_ref[k, 8:9, :] for k in range(CLASSES)], axis=0)
    counts = last[:, FEATS : FEATS + 1]
    mean = last[:, :FEATS] / counts
    mean_ref[...] = mean
    total_weight = jnp.sum(counts, axis=0, keepdims=True)
    lane = lax.broadcasted_iota(jnp.int32, (CLASSES, LANES), 1)
    small = lax.broadcasted_iota(jnp.int32, (CLASSES, FEATS), 1)
    rows_per = LANES // FEATS
    rows = []
    for i in range(FEATS):
        start = (i % rows_per) * FEATS
        part = 2 * (i // rows_per)
        second = jnp.concatenate([sum_ref[part, :8, :], sum_ref[part + 1, :8, :]], axis=0)
        second = second[:, start : start + FEATS]
        spread = second / counts - mean[:, i : i + 1] * mean + jnp.where(small == i, ridge, 0.0)
        unit = jnp.where(small == i, 1.0, 0.0)
        shift = jnp.where(small == 0, mean[:, i : i + 1], 0.0)
        rows.append(jnp.concatenate([unit, shift, spread, jnp.zeros_like(spread)], axis=1))
    diagonal = jnp.ones((CLASSES, LANES), jnp.float32)
    for k in range(FEATS):
        pivot = jnp.sqrt(rows[k][:, 64 + k : 65 + k])
        diagonal = jnp.where(lane == k, pivot, diagonal)
        row = rows[k] * (1.0 / pivot)
        rows[k] = row
        for i in range(k + 1, FEATS):
            rows[i] = rows[i] - row[:, 64 + i : 65 + i] * row
    logdet = jnp.sum(jnp.log(diagonal), axis=1, keepdims=True)
    bias_ref[...] = jnp.broadcast_to(jnp.log(counts / total_weight) - logdet, (CLASSES, LANES))
    for g in range(FEATS):
        offset = -rows[g][:, FEATS : FEATS + 1]
        high = offset.astype(jnp.bfloat16).astype(jnp.float32)
        middle = (offset - high).astype(jnp.bfloat16).astype(jnp.float32)
        low = offset - high - middle
        tail = jnp.where(lane == 34, low, 0.0)
        tail = jnp.where(lane == 33, middle, tail)
        tail = jnp.where(lane == 32, high, tail)
        value = jnp.where(lane < FEATS, rows[g], tail)
        matrix_ref[g * CLASSES : (g + 1) * CLASSES, :] = value.astype(jnp.bfloat16)


def finish(total):
    return pl.pallas_call(
        finish_kernel,
        name="finish",
        out_shape=(
            jax.ShapeDtypeStruct((FEATS * CLASSES, LANES), jnp.bfloat16),
            jax.ShapeDtypeStruct((CLASSES, LANES), jnp.float32),
            jax.ShapeDtypeStruct((CLASSES, FEATS), jnp.float32),
        ),
        in_specs=[VMEM],
        out_specs=(VMEM,) * 3,
        compiler_params=pltpu.CompilerParams(vmem_limit_bytes=LIMIT),
    )(total)


def fill_padded(padded, q_ref, xlo_ref, xhi_ref, ylo_ref, yhi_ref):
    count_x, count_y = q_ref.shape[0], q_ref.shape[1]
    padded[0, 1 : count_y + 1] = xlo_ref[...]
    padded[count_x + 1, 1 : count_y + 1] = xhi_ref[...]
    for x in range(count_x):
        padded[x + 1, 1 : count_y + 1] = q_ref[x]
        padded[x + 1, 0] = ylo_ref[x]
        padded[x + 1, count_y + 1] = yhi_ref[x]


def near_of(padded, zlo_ref, zhi_ref, x, y, c):
    flat = (GROUP * CLASSES, LANES)

    def block(dx, dy):
        return padded[x + 1 + dx, pl.ds(y + 1 + dy, GROUP)].reshape(flat)

    total = block(1, 0).astype(jnp.float32) + block(-1, 0).astype(jnp.float32)
    total = total + block(0, 1).astype(jnp.float32) + block(0, -1).astype(jnp.float32)
    a = lax.broadcasted_iota(jnp.int32, (LANES, LANES), 0)
    b = lax.broadcasted_iota(jnp.int32, (LANES, LANES), 1)
    shift = jnp.where((a == b + 1) | (a + 1 == b), 1.0, 0.0).astype(jnp.bfloat16)
    total = total + jnp.dot(block(0, 0), shift, preferred_element_type=jnp.float32)
    width = GROUP * CLASSES
    where = pl.ds(pl.multiple_of(c * width, width), width)
    side = lax.broadcasted_iota(jnp.int32, (8, width), 0)
    low = jnp.broadcast_to(zlo_ref[:, where].astype(jnp.float32), (8, width))
    high = jnp.broadcast_to(zhi_ref[:, where].astype(jnp.float32), (8, width))
    column = jnp.transpose(jnp.where(side == 0, low, high))
    lane = lax.broadcasted_iota(jnp.int32, flat, 1)
    edge = jnp.where(lane == LANES - 1, column[:, 1:2], 0.0)
    return total + jnp.where(lane == 0, column[:, 0:1], edge)


def update(scores, near):
    value = (scores + beta_coupling * near).reshape(GROUP, CLASSES, LANES)
    value = jnp.exp(value - jnp.max(value, axis=1, keepdims=True))
    value = value * (1.0 / jnp.sum(value, axis=1, keepdims=True))
    return value.astype(jnp.bfloat16)


def scores_of(f_ref, matrix_ref, bias_ref, x, y):
    bias = bias_ref[...]
    parts = []
    for g in range(0, GROUP, 2):
        pair = jnp.concatenate([f_ref[x, y + g], f_ref[x, y + g + 1]], axis=1)
        pair = augmented(pair)
        total = None
        for m in range(0, FEATS * CLASSES, MATRIX_ROWS):
            white = jnp.dot(
                matrix_ref[m : m + MATRIX_ROWS, :AUG], pair, preferred_element_type=jnp.float32
            )
            white = (white * white).reshape(MATRIX_ROWS // CLASSES, CLASSES, 2 * LANES)
            square = jnp.sum(white, axis=0)
            total = square if total is None else total + square
        parts.append(bias - 0.5 * total[:, :LANES])
        parts.append(bias - 0.5 * total[:, LANES:])
    return jnp.concatenate(parts, axis=0)


def first_kernel(f_ref, m_ref, b_ref, q_ref, xlo, xhi, ylo, yhi, zlo, zhi,
                 out_ref, scores_ref, low_ref, high_ref, padded):
    count_x, count_y = q_ref.shape[0], q_ref.shape[1]
    per_x = count_y // GROUP
    fill_padded(padded, q_ref, xlo, xhi, ylo, yhi)

    def step(c, carry):
        x, y = c // per_x, (c % per_x) * GROUP
        scores = scores_of(f_ref, m_ref, b_ref, x, y)
        scores_ref[x, pl.ds(y, GROUP)] = scores.reshape(GROUP, CLASSES, LANES)
        q = update(scores, near_of(padded, zlo, zhi, x, y, c))
        out_ref[x, pl.ds(y, GROUP)] = q
        face_of(q.reshape(GROUP * CLASSES, LANES), low_ref, high_ref, c)
        return carry

    lax.fori_loop(0, count_x * per_x, step, 0, unroll=UNROLL)


def second_kernel(f_ref, scores_ref, q_ref, xlo, xhi, ylo, yhi, zlo, zhi,
                  out_ref, sum_ref, low_ref, high_ref, padded, total):
    count_x, count_y = q_ref.shape[0], q_ref.shape[1]
    per_x = count_y // GROUP
    fill_padded(padded, q_ref, xlo, xhi, ylo, yhi)
    total[...] = jnp.zeros_like(total)

    def step(c, carry):
        x, y = c // per_x, (c % per_x) * GROUP
        scores = scores_ref[x, pl.ds(y, GROUP)].reshape(GROUP * CLASSES, LANES)
        q = update(scores, near_of(padded, zlo, zhi, x, y, c))
        out_ref[x, pl.ds(y, GROUP)] = q
        rows = [f_ref[x, y + g] for g in range(GROUP)]
        add_moments(rows, [q[g] for g in range(GROUP)], total)
        face_of(q.reshape(GROUP * CLASSES, LANES), low_ref, high_ref, c)
        return carry

    lax.fori_loop(0, count_x * per_x, step, 0, unroll=UNROLL)
    pack_moments(total, sum_ref)


def last_kernel(f_ref, m_ref, b_ref, q_ref, xlo, xhi, ylo, yhi, zlo, zhi, out_ref, padded):
    count_x, count_y = q_ref.shape[0], q_ref.shape[1]
    per_x = count_y // GROUP
    fill_padded(padded, q_ref, xlo, xhi, ylo, yhi)

    def step(c, carry):
        x, y = c // per_x, (c % per_x) * GROUP
        scores = scores_of(f_ref, m_ref, b_ref, x, y)
        out_ref[x, pl.ds(y, GROUP)] = update(scores, near_of(padded, zlo, zhi, x, y, c))
        return carry

    lax.fori_loop(0, count_x * per_x, step, 0, unroll=UNROLL)


def sweep_call(kernel, name, operands, q, out_shape, scratch=()):
    count_x, count_y = q.shape[0], q.shape[1]
    padded = pltpu.VMEM((count_x + 2, count_y + 2, CLASSES, LANES), jnp.bfloat16)
    return pl.pallas_call(
        kernel,
        name=name,
        out_shape=out_shape,
        in_specs=[VMEM] * len(operands),
        out_specs=jax.tree.map(lambda _: VMEM, out_shape),
        scratch_shapes=[padded] + list(scratch),
        compiler_params=pltpu.CompilerParams(vmem_limit_bytes=LIMIT),
    )(*operands)


def local(features, posteriors):
    f = features.transpose(1, 2, 0, 3)
    q = posteriors.transpose(1, 2, 0, 3)
    face = jax.ShapeDtypeStruct((1, q.shape[0] * q.shape[1] * CLASSES), jnp.bfloat16)
    state = jax.ShapeDtypeStruct(q.shape, jnp.bfloat16)
    scores_shape = jax.ShapeDtypeStruct(q.shape, jnp.float32)
    sums = jax.ShapeDtypeStruct((PIECES, PIECE_ROWS, LANES), jnp.float32)
    total = pltpu.VMEM((CLASSES * FEATS + CLASSES, LANES), jnp.float32)

    part, low, high = moments(f, q)
    total_sum, halo = summed(part, q, low, high)
    matrix, bias, _ = finish(total_sum)
    q, scores, low, high = sweep_call(
        first_kernel, "first_sweep", [f, matrix, bias, q, *halo], q,
        (state, scores_shape, face, face))
    halo = halo_of(q, low, high)
    q, part, low, high = sweep_call(
        second_kernel, "second_sweep", [f, scores, q, *halo], q,
        (state, sums, face, face), [total])
    total_sum, halo = summed(part, q, low, high)
    matrix, bias, mean = finish(total_sum)
    q = sweep_call(last_kernel, "last_update", [f, matrix, bias, q, *halo], q, state)
    return (q.transpose(2, 0, 1, 3), mean)


def solution(mesh):
    placed = P(None, "gx", "gy", "gz")
    return jax.shard_map(
        local,
        mesh=mesh,
        in_specs=(placed, placed),
        out_specs=(placed, P()),
        check_vma=False,
    )
```

```python
import functools

import jax
import jax.numpy as jnp
from jax import lax
from jax.experimental import pallas as pl
from jax.experimental.pallas import tpu as pltpu
from jax.sharding import PartitionSpec as P

SWEEPS = 2
FEATS = 32
CLASSES = 16
LANES = 128
GROUP = 8
PIECES = 16
PIECE_ROWS = 9
HALVES = 2
AUG = 48

UNROLL = 8
LIMIT = 20 << 20
MATRIX_ROWS = 128

beta_coupling = 1.0
ridge = 0.1

AXES = ("gx", "gy", "gz")
MESH = pl.DeviceIdType.MESH
VMEM = pl.BlockSpec(memory_space=pltpu.VMEM)
NT = (((1,), (1,)), ((), ()))


def augmented(rows):
    count = rows.shape[1]
    index = lax.broadcasted_iota(jnp.int32, (AUG - FEATS, count), 0)
    extra = jnp.where(index < 3, 1.0, 0.0).astype(jnp.bfloat16)
    return jnp.concatenate([rows, extra], axis=0)


def store_faces(q_ref, low_ref, high_ref):
    side = lax.broadcasted_iota(jnp.int32, (16, LANES), 0)
    lane = lax.broadcasted_iota(jnp.int32, (16, LANES), 1)
    pick = ((side == 0) & (lane == 0)) | ((side == 1) & (lane == LANES - 1))
    pick = jnp.where(pick, 1.0, 0.0).astype(jnp.bfloat16)
    width = q_ref.shape[1] * CLASSES
    for x in range(q_ref.shape[0]):
        rows = q_ref[x].reshape(width, LANES)
        faces = lax.dot_general(pick, rows, NT, preferred_element_type=jnp.float32)
        low_ref[:, x * width : (x + 1) * width] = faces[0:1].astype(jnp.bfloat16)
        high_ref[:, x * width : (x + 1) * width] = faces[1:2].astype(jnp.bfloat16)


def add_moments(rows, posts, total):
    weighted = []
    for row, post in zip(rows, posts):
        parts = [post[k : k + 1, :] * row for k in range(CLASSES)] + [post]
        weighted.append(jnp.concatenate(parts, axis=0))
    left = jnp.concatenate(weighted, axis=1)
    right = augmented(jnp.concatenate(rows, axis=1))
    total[:, :AUG] += lax.dot_general(left, right, NT, preferred_element_type=jnp.float32)


def pack_moments(total, out_ref):
    rows_per = LANES // FEATS
    for part in range(FEATS // rows_per):
        blocks = []
        for r in range(rows_per):
            row = part * rows_per + r
            blocks.append(total[pl.ds(row, CLASSES, stride=FEATS), :][:, :FEATS])
        block = jnp.concatenate(blocks, axis=1)
        out_ref[2 * part, :8, :] = block[:8]
        out_ref[2 * part + 1, :8, :] = block[8:]
    for k in range(CLASSES):
        start = CLASSES * FEATS + k
        out_ref[k, 8:9, :] = total[start : start + 1, :]


def moments_kernel(f_ref, q_ref, out_ref, low_ref, high_ref, total):
    count_x, count_y = q_ref.shape[0], q_ref.shape[1]
    per_x = count_y // GROUP
    total[...] = jnp.zeros_like(total)

    def step(c, carry):
        x, y = c // per_x, (c % per_x) * GROUP
        rows = [f_ref[x, y + g] for g in range(GROUP)]
        posts = [q_ref[x, y + g] for g in range(GROUP)]
        add_moments(rows, posts, total)
        return carry

    lax.fori_loop(0, count_x * per_x, step, 0, unroll=UNROLL)
    store_faces(q_ref, low_ref, high_ref)
    pack_moments(total, out_ref)


def moments(f, q):
    faces = q.shape[0] * q.shape[1] * CLASSES
    return pl.pallas_call(
        moments_kernel,
        name="moments",
        out_shape=(
            jax.ShapeDtypeStruct((PIECES, PIECE_ROWS, LANES), jnp.float32),
            jax.ShapeDtypeStruct((1, faces), jnp.bfloat16),
            jax.ShapeDtypeStruct((1, faces), jnp.bfloat16),
        ),
        in_specs=[VMEM] * 2,
        out_specs=(VMEM,) * 3,
        compiler_params=pltpu.CompilerParams(vmem_limit_bytes=LIMIT),
        scratch_shapes=[pltpu.VMEM((CLASSES * FEATS + CLASSES, LANES), jnp.float32)],
    )(f, q)


def places(sizes):
    gx, gy, gz = (lax.axis_index(axis) for axis in AXES)
    depth = sizes["gz"] // HALVES
    half, y = lax.div(gz, depth), lax.rem(gz, depth)
    ring, plane = gy * HALVES + half, gx * depth + y
    rings, planes = sizes["gy"] * HALVES, sizes["gx"] * depth

    def in_ring(d):
        there = lax.rem(ring + d, rings)
        return there, {
            "gy": lax.div(there, HALVES),
            "gz": lax.rem(there, HALVES) * depth + y,
        }

    def in_plane(d):
        there = lax.rem(plane + d, planes)
        return there, {"gx": lax.div(there, depth), "gz": half * depth + lax.rem(there, depth)}

    return (ring, rings, in_ring), (plane, planes, in_plane)


def beside(sizes, axis, d):
    return {axis: lax.rem(lax.axis_index(axis) + d + sizes[axis], sizes[axis])}


def meet(devices):
    barrier = pltpu.get_barrier_semaphore()
    for device in devices:
        pl.semaphore_signal(barrier, inc=1, device_id=device, device_id_type=MESH)
    pl.semaphore_wait(barrier, len(devices))


def remote(source, target, send, recv, device):
    copy = pltpu.make_async_remote_copy(
        src_ref=source, dst_ref=target, send_sem=send, recv_sem=recv,
        device_id=device, device_id_type=MESH,
    )
    copy.start()
    return copy


def start_halo(sizes, q_ref, low_ref, high_ref, halo, send, recv):
    last_x, last_y = q_ref.shape[0] - 1, q_ref.shape[1] - 1
    faces = {
        "gz": (low_ref, high_ref),
        "gx": (q_ref.at[0], q_ref.at[last_x]),
        "gy": (q_ref.at[:, 0], q_ref.at[:, last_y]),
    }
    copies = []
    for axis, (first, last) in faces.items():
        up, down = 2 * AXES.index(axis), 2 * AXES.index(axis) + 1
        copies.append(
            remote(last, halo[up], send.at[up], recv.at[up], beside(sizes, axis, 1))
        )
        copies.append(
            remote(first, halo[down], send.at[down], recv.at[down], beside(sizes, axis, -1))
        )
    return copies


def end_halo(sizes, copies, halo):
    for copy in copies:
        copy.wait()
    for n, axis in enumerate(AXES):
        for ref, edge in ((halo[2 * n], 0), (halo[2 * n + 1], sizes[axis] - 1)):

            @pl.when(lax.axis_index(axis) == edge)
            def _(ref=ref):
                ref[...] = jnp.zeros_like(ref)


def halo_kernel(sizes, q_ref, low_ref, high_ref, *rest):
    halo, (send, recv) = rest[:6], rest[6:]
    meet([beside(sizes, axis, d) for axis in AXES for d in (1, -1)])
    end_halo(sizes, start_halo(sizes, q_ref, low_ref, high_ref, halo, send, recv), halo)


def sum_kernel(sizes, part_ref, q_ref, low_ref, high_ref, out_ref, *rest):
    halo, (held, planar, full, send, recv, halo_send, halo_recv) = rest[:6], rest[6:]
    (ring, rings, in_ring), (plane, planes, in_plane) = places(sizes)
    devices = [in_ring(d)[1] for d in range(1, rings)]
    devices += [in_plane(d)[1] for d in range(1, planes)]
    meet(devices + [beside(sizes, "gz", 1), beside(sizes, "gz", -1)])
    group = PIECES // rings

    def added(ref, count):
        value = ref[0]
        for i in range(1, count):
            value = value + ref[i]
        return value

    held[ring] = part_ref[pl.ds(ring * group, group)]
    copies = []
    for d in range(1, rings):
        there, device = in_ring(d)
        source = part_ref.at[pl.ds(there * group, group)]
        copies.append(remote(source, held.at[ring], send.at[0, d], recv.at[0, d], device))
    halo_copies = start_halo(sizes, q_ref, low_ref, high_ref, halo, halo_send, halo_recv)
    for copy in copies:
        copy.wait()
    planar[plane] = added(held, rings)
    copies = []
    for d in range(1, planes):
        _, device = in_plane(d)
        place = planar.at[plane]
        copies.append(remote(place, place, send.at[1, d], recv.at[1, d], device))
    for copy in copies:
        copy.wait()
    full[ring] = added(planar, planes)
    copies = []
    for d in range(1, rings):
        _, device = in_ring(d)
        place = full.at[ring]
        copies.append(remote(place, place, send.at[2, d], recv.at[2, d], device))
    for copy in copies:
        copy.wait()
    for i in range(rings):
        out_ref[i * group : (i + 1) * group] = full[i]
    end_halo(sizes, halo_copies, halo)


def halo_shapes(q, low):
    plane_x = jax.ShapeDtypeStruct(q.shape[1:], q.dtype)
    plane_y = jax.ShapeDtypeStruct((q.shape[0],) + q.shape[2:], q.dtype)
    plane_z = jax.ShapeDtypeStruct(low.shape, low.dtype)
    return (plane_x, plane_x, plane_y, plane_y, plane_z, plane_z)


def halo_of(q, low, high):
    sizes = {axis: lax.axis_size(axis) for axis in AXES}
    return pl.pallas_call(
        functools.partial(halo_kernel, sizes),
        name="halo",
        out_shape=halo_shapes(q, low),
        in_specs=[VMEM] * 3,
        out_specs=(VMEM,) * 6,
        scratch_shapes=[pltpu.SemaphoreType.DMA((6,)), pltpu.SemaphoreType.DMA((6,))],
        compiler_params=pltpu.CompilerParams(collective_id=1, vmem_limit_bytes=LIMIT, has_side_effects=True),
    )(q, low, high)


def summed(part, q, low, high):
    sizes = {axis: lax.axis_size(axis) for axis in AXES}
    rings, planes = sizes["gy"] * HALVES, sizes["gx"] * (sizes["gz"] // HALVES)
    block = (PIECES // rings, PIECE_ROWS, LANES)
    most = max(rings, planes)
    total, *halo = pl.pallas_call(
        functools.partial(sum_kernel, sizes),
        name="sum_and_halo",
        out_shape=(jax.ShapeDtypeStruct(part.shape, jnp.float32),) + halo_shapes(q, low),
        in_specs=[VMEM] * 4,
        out_specs=(VMEM,) * 7,
        scratch_shapes=[
            pltpu.VMEM((rings,) + block, jnp.float32),
            pltpu.VMEM((planes,) + block, jnp.float32),
            pltpu.VMEM((rings,) + block, jnp.float32),
            pltpu.SemaphoreType.DMA((3, most)),
            pltpu.SemaphoreType.DMA((3, most)),
            pltpu.SemaphoreType.DMA((6,)),
            pltpu.SemaphoreType.DMA((6,)),
        ],
        compiler_params=pltpu.CompilerParams(collective_id=0, vmem_limit_bytes=LIMIT, has_side_effects=True),
    )(part, q, low, high)
    return total, halo


def finish_kernel(sum_ref, matrix_ref, bias_ref, mean_ref):
    last = jnp.concatenate([sum_ref[k, 8:9, :] for k in range(CLASSES)], axis=0)
    counts = last[:, FEATS : FEATS + 1]
    mean = last[:, :FEATS] / counts
    mean_ref[...] = mean
    total_weight = jnp.sum(counts, axis=0, keepdims=True)
    lane = lax.broadcasted_iota(jnp.int32, (CLASSES, LANES), 1)
    small = lax.broadcasted_iota(jnp.int32, (CLASSES, FEATS), 1)
    rows_per = LANES // FEATS
    rows = []
    for i in range(FEATS):
        start = (i % rows_per) * FEATS
        part = 2 * (i // rows_per)
        second = jnp.concatenate([sum_ref[part, :8, :], sum_ref[part + 1, :8, :]], axis=0)
        second = second[:, start : start + FEATS]
        spread = second / counts - mean[:, i : i + 1] * mean + jnp.where(small == i, ridge, 0.0)
        unit = jnp.where(small == i, 1.0, 0.0)
        shift = jnp.where(small == 0, mean[:, i : i + 1], 0.0)
        rows.append(jnp.concatenate([unit, shift, spread, jnp.zeros_like(spread)], axis=1))
    diagonal = jnp.ones((CLASSES, LANES), jnp.float32)
    for k in range(FEATS):
        row = rows[k]
        square = jnp.broadcast_to(row[:, 64 + k : 65 + k], row.shape)
        inverse = 1.0 / square
        for i in range(k + 1, FEATS):
            rows[i] = rows[i] - (row[:, 64 + i : 65 + i] * inverse) * row
        pivot = jnp.sqrt(square)
        diagonal = jnp.where(lane == k, pivot, diagonal)
        rows[k] = row * (1.0 / pivot)
    logdet = jnp.sum(jnp.log(diagonal), axis=1, keepdims=True)
    bias_ref[...] = jnp.broadcast_to(jnp.log(counts / total_weight) - logdet, (CLASSES, LANES))
    for g in range(FEATS):
        offset = -rows[g][:, FEATS : FEATS + 1]
        high = offset.astype(jnp.bfloat16).astype(jnp.float32)
        middle = (offset - high).astype(jnp.bfloat16).astype(jnp.float32)
        low = offset - high - middle
        tail = jnp.where(lane == 34, low, 0.0)
        tail = jnp.where(lane == 33, middle, tail)
        tail = jnp.where(lane == 32, high, tail)
        value = jnp.where(lane < FEATS, rows[g], tail)
        matrix_ref[g * CLASSES : (g + 1) * CLASSES, :] = value.astype(jnp.bfloat16)


def finish(total):
    return pl.pallas_call(
        finish_kernel,
        name="finish",
        out_shape=(
            jax.ShapeDtypeStruct((FEATS * CLASSES, LANES), jnp.bfloat16),
            jax.ShapeDtypeStruct((CLASSES, LANES), jnp.float32),
            jax.ShapeDtypeStruct((CLASSES, FEATS), jnp.float32),
        ),
        in_specs=[VMEM],
        out_specs=(VMEM,) * 3,
        compiler_params=pltpu.CompilerParams(vmem_limit_bytes=LIMIT),
    )(total)


def fill_padded(padded, q_ref, xlo_ref, xhi_ref, ylo_ref, yhi_ref):
    count_x, count_y = q_ref.shape[0], q_ref.shape[1]
    padded[0, 1 : count_y + 1] = xlo_ref[...]
    padded[count_x + 1, 1 : count_y + 1] = xhi_ref[...]
    for x in range(count_x):
        padded[x + 1, 1 : count_y + 1] = q_ref[x]
        padded[x + 1, 0] = ylo_ref[x]
        padded[x + 1, count_y + 1] = yhi_ref[x]


def near_of(padded, zlo_ref, zhi_ref, x, y, c):
    flat = (GROUP * CLASSES, LANES)

    def block(dx, dy):
        return padded[x + 1 + dx, pl.ds(y + 1 + dy, GROUP)].reshape(flat)

    total = block(1, 0).astype(jnp.float32) + block(-1, 0).astype(jnp.float32)
    total = total + block(0, 1).astype(jnp.float32) + block(0, -1).astype(jnp.float32)
    a = lax.broadcasted_iota(jnp.int32, (LANES, LANES), 0)
    b = lax.broadcasted_iota(jnp.int32, (LANES, LANES), 1)
    shift = jnp.where((a == b + 1) | (a + 1 == b), 1.0, 0.0).astype(jnp.bfloat16)
    total = total + jnp.dot(block(0, 0), shift, preferred_element_type=jnp.float32)
    width = GROUP * CLASSES
    where = pl.ds(pl.multiple_of(c * width, width), width)
    side = lax.broadcasted_iota(jnp.int32, (8, width), 0)
    low = jnp.broadcast_to(zlo_ref[:, where].astype(jnp.float32), (8, width))
    high = jnp.broadcast_to(zhi_ref[:, where].astype(jnp.float32), (8, width))
    column = jnp.transpose(jnp.where(side == 0, low, high))
    lane = lax.broadcasted_iota(jnp.int32, flat, 1)
    edge = jnp.where(lane == LANES - 1, column[:, 1:2], 0.0)
    return total + jnp.where(lane == 0, column[:, 0:1], edge)


def update(scores, near):
    value = (scores + beta_coupling * near).reshape(GROUP, CLASSES, LANES)
    value = jnp.exp(value - jnp.max(value, axis=1, keepdims=True))
    value = value * (1.0 / jnp.sum(value, axis=1, keepdims=True))
    return value.astype(jnp.bfloat16)


def scores_of(f_ref, matrix_ref, bias_ref, x, y):
    bias = bias_ref[...]
    parts = []
    for g in range(0, GROUP, 2):
        pair = jnp.concatenate([f_ref[x, y + g], f_ref[x, y + g + 1]], axis=1)
        pair = augmented(pair)
        total = None
        for m in range(0, FEATS * CLASSES, MATRIX_ROWS):
            white = jnp.dot(
                matrix_ref[m : m + MATRIX_ROWS, :AUG], pair, preferred_element_type=jnp.float32
            )
            white = (white * white).reshape(MATRIX_ROWS // CLASSES, CLASSES, 2 * LANES)
            square = jnp.sum(white, axis=0)
            total = square if total is None else total + square
        parts.append(bias - 0.5 * total[:, :LANES])
        parts.append(bias - 0.5 * total[:, LANES:])
    return jnp.concatenate(parts, axis=0)


def first_kernel(f_ref, m_ref, b_ref, q_ref, xlo, xhi, ylo, yhi, zlo, zhi,
                 out_ref, scores_ref, low_ref, high_ref, padded):
    count_x, count_y = q_ref.shape[0], q_ref.shape[1]
    per_x = count_y // GROUP
    fill_padded(padded, q_ref, xlo, xhi, ylo, yhi)

    def step(c, carry):
        x, y = c // per_x, (c % per_x) * GROUP
        scores = scores_of(f_ref, m_ref, b_ref, x, y)
        scores_ref[x, pl.ds(y, GROUP)] = scores.reshape(GROUP, CLASSES, LANES)
        q = update(scores, near_of(padded, zlo, zhi, x, y, c))
        out_ref[x, pl.ds(y, GROUP)] = q
        return carry

    lax.fori_loop(0, count_x * per_x, step, 0, unroll=UNROLL)
    store_faces(out_ref, low_ref, high_ref)


def second_kernel(f_ref, scores_ref, q_ref, xlo, xhi, ylo, yhi, zlo, zhi,
                  out_ref, sum_ref, low_ref, high_ref, padded, total):
    count_x, count_y = q_ref.shape[0], q_ref.shape[1]
    per_x = count_y // GROUP
    fill_padded(padded, q_ref, xlo, xhi, ylo, yhi)
    total[...] = jnp.zeros_like(total)

    def step(c, carry):
        x, y = c // per_x, (c % per_x) * GROUP
        scores = scores_ref[x, pl.ds(y, GROUP)].reshape(GROUP * CLASSES, LANES)
        q = update(scores, near_of(padded, zlo, zhi, x, y, c))
        out_ref[x, pl.ds(y, GROUP)] = q
        rows = [f_ref[x, y + g] for g in range(GROUP)]
        add_moments(rows, [q[g] for g in range(GROUP)], total)
        return carry

    lax.fori_loop(0, count_x * per_x, step, 0, unroll=UNROLL)
    store_faces(out_ref, low_ref, high_ref)
    pack_moments(total, sum_ref)


def last_kernel(f_ref, m_ref, b_ref, q_ref, xlo, xhi, ylo, yhi, zlo, zhi, out_ref, padded):
    count_x, count_y = q_ref.shape[0], q_ref.shape[1]
    per_x = count_y // GROUP
    fill_padded(padded, q_ref, xlo, xhi, ylo, yhi)

    def step(c, carry):
        x, y = c // per_x, (c % per_x) * GROUP
        scores = scores_of(f_ref, m_ref, b_ref, x, y)
        out_ref[x, pl.ds(y, GROUP)] = update(scores, near_of(padded, zlo, zhi, x, y, c))
        return carry

    lax.fori_loop(0, count_x * per_x, step, 0, unroll=UNROLL)


def sweep_call(kernel, name, operands, q, out_shape, scratch=()):
    count_x, count_y = q.shape[0], q.shape[1]
    padded = pltpu.VMEM((count_x + 2, count_y + 2, CLASSES, LANES), jnp.bfloat16)
    return pl.pallas_call(
        kernel,
        name=name,
        out_shape=out_shape,
        in_specs=[VMEM] * len(operands),
        out_specs=jax.tree.map(lambda _: VMEM, out_shape),
        scratch_shapes=[padded] + list(scratch),
        compiler_params=pltpu.CompilerParams(vmem_limit_bytes=LIMIT),
    )(*operands)


def local(features, posteriors):
    f = features.transpose(1, 2, 0, 3)
    q = posteriors.transpose(1, 2, 0, 3)
    face = jax.ShapeDtypeStruct((1, q.shape[0] * q.shape[1] * CLASSES), jnp.bfloat16)
    state = jax.ShapeDtypeStruct(q.shape, jnp.bfloat16)
    scores_shape = jax.ShapeDtypeStruct(q.shape, jnp.float32)
    sums = jax.ShapeDtypeStruct((PIECES, PIECE_ROWS, LANES), jnp.float32)
    total = pltpu.VMEM((CLASSES * FEATS + CLASSES, LANES), jnp.float32)

    part, low, high = moments(f, q)
    total_sum, halo = summed(part, q, low, high)
    matrix, bias, _ = finish(total_sum)
    q, scores, low, high = sweep_call(
        first_kernel, "first_sweep", [f, matrix, bias, q, *halo], q,
        (state, scores_shape, face, face))
    halo = halo_of(q, low, high)
    q, part, low, high = sweep_call(
        second_kernel, "second_sweep", [f, scores, q, *halo], q,
        (state, sums, face, face), [total])
    total_sum, halo = summed(part, q, low, high)
    matrix, bias, mean = finish(total_sum)
    q = sweep_call(last_kernel, "last_update", [f, matrix, bias, q, *halo], q, state)
    return (q.transpose(2, 0, 1, 3), mean)


def solution(mesh):
    placed = P(None, "gx", "gy", "gz")
    return jax.shard_map(
        local,
        mesh=mesh,
        in_specs=(placed, placed),
        out_specs=(placed, P()),
        check_vma=False,
    )
```

```python
import functools

import jax
import jax.numpy as jnp
from jax import lax
from jax.experimental import pallas as pl
from jax.experimental.pallas import tpu as pltpu
from jax.sharding import PartitionSpec as P

SWEEPS = 2
FEATS = 32
CLASSES = 16
LANES = 128
GROUP = 8
PIECES = 16
PIECE_ROWS = 9
HALVES = 2
AUG = 48

UNROLL = 8
LIMIT = 20 << 20
MATRIX_ROWS = 128

beta_coupling = 1.0
ridge = 0.1

AXES = ("gx", "gy", "gz")
MESH = pl.DeviceIdType.MESH
VMEM = pl.BlockSpec(memory_space=pltpu.VMEM)
NT = (((1,), (1,)), ((), ()))


def augmented(rows):
    count = rows.shape[1]
    index = lax.broadcasted_iota(jnp.int32, (AUG - FEATS, count), 0)
    extra = jnp.where(index < 3, 1.0, 0.0).astype(jnp.bfloat16)
    return jnp.concatenate([rows, extra], axis=0)


def store_faces(q_ref, low_ref, high_ref):
    side = lax.broadcasted_iota(jnp.int32, (16, LANES), 0)
    lane = lax.broadcasted_iota(jnp.int32, (16, LANES), 1)
    pick = ((side == 0) & (lane == 0)) | ((side == 1) & (lane == LANES - 1))
    pick = jnp.where(pick, 1.0, 0.0).astype(jnp.bfloat16)
    width = q_ref.shape[1] * CLASSES
    for x in range(q_ref.shape[0]):
        rows = q_ref[x].reshape(width, LANES)
        faces = lax.dot_general(pick, rows, NT, preferred_element_type=jnp.float32)
        low_ref[:, x * width : (x + 1) * width] = faces[0:1].astype(jnp.bfloat16)
        high_ref[:, x * width : (x + 1) * width] = faces[1:2].astype(jnp.bfloat16)


def add_moments(rows, posts, total):
    weighted = []
    for row, post in zip(rows, posts):
        parts = [post[k : k + 1, :] * row for k in range(CLASSES)] + [post]
        weighted.append(jnp.concatenate(parts, axis=0))
    left = jnp.concatenate(weighted, axis=1)
    right = augmented(jnp.concatenate(rows, axis=1))
    total[:, :AUG] += lax.dot_general(left, right, NT, preferred_element_type=jnp.float32)


def pack_moments(total, out_ref):
    rows_per = LANES // FEATS
    for part in range(FEATS // rows_per):
        blocks = []
        for r in range(rows_per):
            row = part * rows_per + r
            blocks.append(total[pl.ds(row, CLASSES, stride=FEATS), :][:, :FEATS])
        block = jnp.concatenate(blocks, axis=1)
        out_ref[2 * part, :8, :] = block[:8]
        out_ref[2 * part + 1, :8, :] = block[8:]
    for k in range(CLASSES):
        start = CLASSES * FEATS + k
        out_ref[k, 8:9, :] = total[start : start + 1, :]


def moments_kernel(f_ref, q_ref, out_ref, low_ref, high_ref, total):
    count_x, count_y = q_ref.shape[0], q_ref.shape[1]
    per_x = count_y // GROUP
    total[...] = jnp.zeros_like(total)

    def step(c, carry):
        x, y = c // per_x, (c % per_x) * GROUP
        rows = [f_ref[x, y + g] for g in range(GROUP)]
        posts = [q_ref[x, y + g] for g in range(GROUP)]
        add_moments(rows, posts, total)
        return carry

    lax.fori_loop(0, count_x * per_x, step, 0, unroll=UNROLL)
    store_faces(q_ref, low_ref, high_ref)
    pack_moments(total, out_ref)


def moments(f, q):
    faces = q.shape[0] * q.shape[1] * CLASSES
    return pl.pallas_call(
        moments_kernel,
        name="moments",
        out_shape=(
            jax.ShapeDtypeStruct((PIECES, PIECE_ROWS, LANES), jnp.float32),
            jax.ShapeDtypeStruct((1, faces), jnp.bfloat16),
            jax.ShapeDtypeStruct((1, faces), jnp.bfloat16),
        ),
        in_specs=[VMEM] * 2,
        out_specs=(VMEM,) * 3,
        compiler_params=pltpu.CompilerParams(vmem_limit_bytes=LIMIT),
        scratch_shapes=[pltpu.VMEM((CLASSES * FEATS + CLASSES, LANES), jnp.float32)],
    )(f, q)


def places(sizes):
    gx, gy, gz = (lax.axis_index(axis) for axis in AXES)
    depth = sizes["gz"] // HALVES
    half, y = lax.div(gz, depth), lax.rem(gz, depth)
    ring, plane = gy * HALVES + half, gx * depth + y
    rings, planes = sizes["gy"] * HALVES, sizes["gx"] * depth

    def in_ring(d):
        there = lax.rem(ring + d, rings)
        return there, {
            "gy": lax.div(there, HALVES),
            "gz": lax.rem(there, HALVES) * depth + y,
        }

    def in_plane(d):
        there = lax.rem(plane + d, planes)
        return there, {"gx": lax.div(there, depth), "gz": half * depth + lax.rem(there, depth)}

    return (ring, rings, in_ring), (plane, planes, in_plane)


def beside(sizes, axis, d):
    return {axis: lax.rem(lax.axis_index(axis) + d + sizes[axis], sizes[axis])}


def greet(devices):
    barrier = pltpu.get_barrier_semaphore()
    for device in devices:
        pl.semaphore_signal(barrier, inc=1, device_id=device, device_id_type=MESH)
    return barrier


def meet(devices):
    pl.semaphore_wait(greet(devices), len(devices))


def remote(source, target, send, recv, device):
    copy = pltpu.make_async_remote_copy(
        src_ref=source, dst_ref=target, send_sem=send, recv_sem=recv,
        device_id=device, device_id_type=MESH,
    )
    copy.start()
    return copy


def start_halo(sizes, q_ref, low_ref, high_ref, halo, send, recv):
    last_x, last_y = q_ref.shape[0] - 1, q_ref.shape[1] - 1
    faces = {
        "gz": (low_ref, high_ref),
        "gx": (q_ref.at[0], q_ref.at[last_x]),
        "gy": (q_ref.at[:, 0], q_ref.at[:, last_y]),
    }
    copies = []
    for axis, (first, last) in faces.items():
        up, down = 2 * AXES.index(axis), 2 * AXES.index(axis) + 1
        copies.append(
            remote(last, halo[up], send.at[up], recv.at[up], beside(sizes, axis, 1))
        )
        copies.append(
            remote(first, halo[down], send.at[down], recv.at[down], beside(sizes, axis, -1))
        )
    return copies


def end_halo(sizes, copies, halo):
    for copy in copies:
        copy.wait()
    for n, axis in enumerate(AXES):
        for ref, edge in ((halo[2 * n], 0), (halo[2 * n + 1], sizes[axis] - 1)):

            @pl.when(lax.axis_index(axis) == edge)
            def _(ref=ref):
                ref[...] = jnp.zeros_like(ref)


def sum_kernel(sizes, part_ref, q_ref, low_ref, high_ref, out_ref, *rest):
    halo, (held, planar, full, send, recv, halo_send, halo_recv) = rest[:6], rest[6:]
    (ring, rings, in_ring), (plane, planes, in_plane) = places(sizes)
    devices = [in_ring(d)[1] for d in range(1, rings)]
    devices += [in_plane(d)[1] for d in range(1, planes)]
    meet(devices + [beside(sizes, "gz", 1), beside(sizes, "gz", -1)])
    group = PIECES // rings

    def added(ref, count):
        value = ref[0]
        for i in range(1, count):
            value = value + ref[i]
        return value

    held[ring] = part_ref[pl.ds(ring * group, group)]
    copies = []
    for d in range(1, rings):
        there, device = in_ring(d)
        source = part_ref.at[pl.ds(there * group, group)]
        copies.append(remote(source, held.at[ring], send.at[0, d], recv.at[0, d], device))
    halo_copies = start_halo(sizes, q_ref, low_ref, high_ref, halo, halo_send, halo_recv)
    for copy in copies:
        copy.wait()
    planar[plane] = added(held, rings)
    copies = []
    for d in range(1, planes):
        _, device = in_plane(d)
        place = planar.at[plane]
        copies.append(remote(place, place, send.at[1, d], recv.at[1, d], device))
    for copy in copies:
        copy.wait()
    full[ring] = added(planar, planes)
    copies = []
    for d in range(1, rings):
        _, device = in_ring(d)
        place = full.at[ring]
        copies.append(remote(place, place, send.at[2, d], recv.at[2, d], device))
    for copy in copies:
        copy.wait()
    for i in range(rings):
        out_ref[i * group : (i + 1) * group] = full[i]
    end_halo(sizes, halo_copies, halo)


def halo_shapes(q, low):
    plane_x = jax.ShapeDtypeStruct(q.shape[1:], q.dtype)
    plane_y = jax.ShapeDtypeStruct((q.shape[0],) + q.shape[2:], q.dtype)
    plane_z = jax.ShapeDtypeStruct(low.shape, low.dtype)
    return (plane_x, plane_x, plane_y, plane_y, plane_z, plane_z)


def summed(part, q, low, high):
    sizes = {axis: lax.axis_size(axis) for axis in AXES}
    rings, planes = sizes["gy"] * HALVES, sizes["gx"] * (sizes["gz"] // HALVES)
    block = (PIECES // rings, PIECE_ROWS, LANES)
    most = max(rings, planes)
    total, *halo = pl.pallas_call(
        functools.partial(sum_kernel, sizes),
        name="sum_and_halo",
        out_shape=(jax.ShapeDtypeStruct(part.shape, jnp.float32),) + halo_shapes(q, low),
        in_specs=[VMEM] * 4,
        out_specs=(VMEM,) * 7,
        scratch_shapes=[
            pltpu.VMEM((rings,) + block, jnp.float32),
            pltpu.VMEM((planes,) + block, jnp.float32),
            pltpu.VMEM((rings,) + block, jnp.float32),
            pltpu.SemaphoreType.DMA((3, most)),
            pltpu.SemaphoreType.DMA((3, most)),
            pltpu.SemaphoreType.DMA((6,)),
            pltpu.SemaphoreType.DMA((6,)),
        ],
        compiler_params=pltpu.CompilerParams(collective_id=0, vmem_limit_bytes=LIMIT, has_side_effects=True),
    )(part, q, low, high)
    return total, halo


def finish_kernel(sum_ref, matrix_ref, bias_ref, mean_ref):
    last = jnp.concatenate([sum_ref[k, 8:9, :] for k in range(CLASSES)], axis=0)
    counts = last[:, FEATS : FEATS + 1]
    mean = last[:, :FEATS] / counts
    mean_ref[...] = mean
    total_weight = jnp.sum(counts, axis=0, keepdims=True)
    lane = lax.broadcasted_iota(jnp.int32, (CLASSES, LANES), 1)
    small = lax.broadcasted_iota(jnp.int32, (CLASSES, FEATS), 1)
    rows_per = LANES // FEATS
    rows = []
    for i in range(FEATS):
        start = (i % rows_per) * FEATS
        part = 2 * (i // rows_per)
        second = jnp.concatenate([sum_ref[part, :8, :], sum_ref[part + 1, :8, :]], axis=0)
        second = second[:, start : start + FEATS]
        spread = second / counts - mean[:, i : i + 1] * mean + jnp.where(small == i, ridge, 0.0)
        unit = jnp.where(small == i, 1.0, 0.0)
        shift = jnp.where(small == 0, mean[:, i : i + 1], 0.0)
        rows.append(jnp.concatenate([unit, shift, spread, jnp.zeros_like(spread)], axis=1))
    diagonal = jnp.ones((CLASSES, LANES), jnp.float32)
    for k in range(FEATS):
        row = rows[k]
        square = jnp.broadcast_to(row[:, 64 + k : 65 + k], row.shape)
        inverse = 1.0 / square
        for i in range(k + 1, FEATS):
            rows[i] = rows[i] - (row[:, 64 + i : 65 + i] * inverse) * row
        pivot = jnp.sqrt(square)
        diagonal = jnp.where(lane == k, pivot, diagonal)
        rows[k] = row * (1.0 / pivot)
    logdet = jnp.sum(jnp.log(diagonal), axis=1, keepdims=True)
    bias_ref[...] = jnp.broadcast_to(jnp.log(counts / total_weight) - logdet, (CLASSES, LANES))
    for g in range(FEATS):
        offset = -rows[g][:, FEATS : FEATS + 1]
        high = offset.astype(jnp.bfloat16).astype(jnp.float32)
        middle = (offset - high).astype(jnp.bfloat16).astype(jnp.float32)
        low = offset - high - middle
        tail = jnp.where(lane == 34, low, 0.0)
        tail = jnp.where(lane == 33, middle, tail)
        tail = jnp.where(lane == 32, high, tail)
        value = jnp.where(lane < FEATS, rows[g], tail)
        matrix_ref[g * CLASSES : (g + 1) * CLASSES, :] = value.astype(jnp.bfloat16)


def finish(total):
    return pl.pallas_call(
        finish_kernel,
        name="finish",
        out_shape=(
            jax.ShapeDtypeStruct((FEATS * CLASSES, LANES), jnp.bfloat16),
            jax.ShapeDtypeStruct((CLASSES, LANES), jnp.float32),
            jax.ShapeDtypeStruct((CLASSES, FEATS), jnp.float32),
        ),
        in_specs=[VMEM],
        out_specs=(VMEM,) * 3,
        compiler_params=pltpu.CompilerParams(vmem_limit_bytes=LIMIT),
    )(total)


def fill_padded(padded, q_ref, xlo_ref, xhi_ref, ylo_ref, yhi_ref):
    count_x, count_y = q_ref.shape[0], q_ref.shape[1]
    padded[0, 1 : count_y + 1] = xlo_ref[...]
    padded[count_x + 1, 1 : count_y + 1] = xhi_ref[...]
    for x in range(count_x):
        padded[x + 1, 1 : count_y + 1] = q_ref[x]
        padded[x + 1, 0] = ylo_ref[x]
        padded[x + 1, count_y + 1] = yhi_ref[x]


def near_of(padded, zlo_ref, zhi_ref, x, y, c):
    flat = (GROUP * CLASSES, LANES)

    def block(dx, dy):
        return padded[x + 1 + dx, pl.ds(y + 1 + dy, GROUP)].reshape(flat)

    total = block(1, 0).astype(jnp.float32) + block(-1, 0).astype(jnp.float32)
    total = total + block(0, 1).astype(jnp.float32) + block(0, -1).astype(jnp.float32)
    a = lax.broadcasted_iota(jnp.int32, (LANES, LANES), 0)
    b = lax.broadcasted_iota(jnp.int32, (LANES, LANES), 1)
    shift = jnp.where((a == b + 1) | (a + 1 == b), 1.0, 0.0).astype(jnp.bfloat16)
    total = total + jnp.dot(block(0, 0), shift, preferred_element_type=jnp.float32)
    width = GROUP * CLASSES
    where = pl.ds(pl.multiple_of(c * width, width), width)
    side = lax.broadcasted_iota(jnp.int32, (8, width), 0)
    low = jnp.broadcast_to(zlo_ref[:, where].astype(jnp.float32), (8, width))
    high = jnp.broadcast_to(zhi_ref[:, where].astype(jnp.float32), (8, width))
    column = jnp.transpose(jnp.where(side == 0, low, high))
    lane = lax.broadcasted_iota(jnp.int32, flat, 1)
    edge = jnp.where(lane == LANES - 1, column[:, 1:2], 0.0)
    return total + jnp.where(lane == 0, column[:, 0:1], edge)


def update(scores, near):
    value = (scores + beta_coupling * near).reshape(GROUP, CLASSES, LANES)
    value = jnp.exp(value - jnp.max(value, axis=1, keepdims=True))
    value = value * (1.0 / jnp.sum(value, axis=1, keepdims=True))
    return value.astype(jnp.bfloat16)


def scores_of(f_ref, matrix_ref, bias_ref, x, y):
    bias = bias_ref[...]
    parts = []
    for g in range(0, GROUP, 2):
        pair = jnp.concatenate([f_ref[x, y + g], f_ref[x, y + g + 1]], axis=1)
        pair = augmented(pair)
        total = None
        for m in range(0, FEATS * CLASSES, MATRIX_ROWS):
            white = jnp.dot(
                matrix_ref[m : m + MATRIX_ROWS, :AUG], pair, preferred_element_type=jnp.float32
            )
            white = (white * white).reshape(MATRIX_ROWS // CLASSES, CLASSES, 2 * LANES)
            square = jnp.sum(white, axis=0)
            total = square if total is None else total + square
        parts.append(bias - 0.5 * total[:, :LANES])
        parts.append(bias - 0.5 * total[:, LANES:])
    return jnp.concatenate(parts, axis=0)


def first_kernel(sizes, f_ref, m_ref, b_ref, q_ref, xlo, xhi, ylo, yhi, zlo, zhi,
                 out_ref, scores_ref, *rest):
    halo, (padded, low_ref, high_ref, send, recv) = rest[:6], rest[6:]
    devices = [beside(sizes, axis, d) for axis in AXES for d in (1, -1)]
    barrier = greet(devices)
    count_x, count_y = q_ref.shape[0], q_ref.shape[1]
    per_x = count_y // GROUP
    fill_padded(padded, q_ref, xlo, xhi, ylo, yhi)

    def step(c, carry):
        x, y = c // per_x, (c % per_x) * GROUP
        scores = scores_of(f_ref, m_ref, b_ref, x, y)
        scores_ref[x, pl.ds(y, GROUP)] = scores.reshape(GROUP, CLASSES, LANES)
        q = update(scores, near_of(padded, zlo, zhi, x, y, c))
        out_ref[x, pl.ds(y, GROUP)] = q
        return carry

    lax.fori_loop(0, count_x * per_x, step, 0, unroll=UNROLL)
    store_faces(out_ref, low_ref, high_ref)
    pl.semaphore_wait(barrier, len(devices))
    end_halo(sizes, start_halo(sizes, out_ref, low_ref, high_ref, halo, send, recv), halo)


def second_kernel(f_ref, scores_ref, q_ref, xlo, xhi, ylo, yhi, zlo, zhi,
                  out_ref, sum_ref, low_ref, high_ref, padded, total):
    count_x, count_y = q_ref.shape[0], q_ref.shape[1]
    per_x = count_y // GROUP
    fill_padded(padded, q_ref, xlo, xhi, ylo, yhi)
    total[...] = jnp.zeros_like(total)

    def step(c, carry):
        x, y = c // per_x, (c % per_x) * GROUP
        scores = scores_ref[x, pl.ds(y, GROUP)].reshape(GROUP * CLASSES, LANES)
        q = update(scores, near_of(padded, zlo, zhi, x, y, c))
        out_ref[x, pl.ds(y, GROUP)] = q
        rows = [f_ref[x, y + g] for g in range(GROUP)]
        add_moments(rows, [q[g] for g in range(GROUP)], total)
        return carry

    lax.fori_loop(0, count_x * per_x, step, 0, unroll=UNROLL)
    store_faces(out_ref, low_ref, high_ref)
    pack_moments(total, sum_ref)


def last_kernel(f_ref, m_ref, b_ref, q_ref, xlo, xhi, ylo, yhi, zlo, zhi, out_ref, padded):
    count_x, count_y = q_ref.shape[0], q_ref.shape[1]
    per_x = count_y // GROUP
    fill_padded(padded, q_ref, xlo, xhi, ylo, yhi)

    def step(c, carry):
        x, y = c // per_x, (c % per_x) * GROUP
        scores = scores_of(f_ref, m_ref, b_ref, x, y)
        out_ref[x, pl.ds(y, GROUP)] = update(scores, near_of(padded, zlo, zhi, x, y, c))
        return carry

    lax.fori_loop(0, count_x * per_x, step, 0, unroll=UNROLL)


def sweep_call(kernel, name, operands, q, out_shape, scratch=(), **params):
    count_x, count_y = q.shape[0], q.shape[1]
    padded = pltpu.VMEM((count_x + 2, count_y + 2, CLASSES, LANES), jnp.bfloat16)
    return pl.pallas_call(
        kernel,
        name=name,
        out_shape=out_shape,
        in_specs=[VMEM] * len(operands),
        out_specs=jax.tree.map(lambda _: VMEM, out_shape),
        scratch_shapes=[padded] + list(scratch),
        compiler_params=pltpu.CompilerParams(vmem_limit_bytes=LIMIT, **params),
    )(*operands)


def local(features, posteriors):
    f = features.transpose(1, 2, 0, 3)
    q = posteriors.transpose(1, 2, 0, 3)
    face = jax.ShapeDtypeStruct((1, q.shape[0] * q.shape[1] * CLASSES), jnp.bfloat16)
    state = jax.ShapeDtypeStruct(q.shape, jnp.bfloat16)
    scores_shape = jax.ShapeDtypeStruct(q.shape, jnp.float32)
    sums = jax.ShapeDtypeStruct((PIECES, PIECE_ROWS, LANES), jnp.float32)
    total = pltpu.VMEM((CLASSES * FEATS + CLASSES, LANES), jnp.float32)

    part, low, high = moments(f, q)
    total_sum, halo = summed(part, q, low, high)
    matrix, bias, _ = finish(total_sum)
    sizes = {axis: lax.axis_size(axis) for axis in AXES}
    semaphores = [pltpu.SemaphoreType.DMA((6,)), pltpu.SemaphoreType.DMA((6,))]
    faces = [pltpu.VMEM(face.shape, face.dtype)] * 2
    q, scores, *halo = sweep_call(
        functools.partial(first_kernel, sizes), "first_sweep", [f, matrix, bias, q, *halo], q,
        (state, scores_shape) + halo_shapes(q, low), faces + semaphores,
        collective_id=1, has_side_effects=True)
    q, part, low, high = sweep_call(
        second_kernel, "second_sweep", [f, scores, q, *halo], q,
        (state, sums, face, face), [total])
    total_sum, halo = summed(part, q, low, high)
    matrix, bias, mean = finish(total_sum)
    q = sweep_call(last_kernel, "last_update", [f, matrix, bias, q, *halo], q, state)
    return (q.transpose(2, 0, 1, 3), mean)


def solution(mesh):
    placed = P(None, "gx", "gy", "gz")
    return jax.shard_map(
        local,
        mesh=mesh,
        in_specs=(placed, placed),
        out_specs=(placed, P()),
        check_vma=False,
    )
```
